256 devices in a mesh: ctx: 64 (over x_hi, z, y), head: 4 (over x_lo, core).
Axes of the slice: x: 4 (x_hi: 2, x_lo: 2; x = x_hi * 2 + x_lo), y: 4, z: 8, core: 2. Of those that a mesh axis runs over, the one named last changes fastest.
Arguments:
- tokens: bfloat16 [16384, 1024], P('ctx', 'head')
- gain: float32 [1024], replicated, may hold values from 0.25 to 1.75
- w_query: bfloat16 [1024, 1024], P(None, 'head'), may hold values from -0.1875 to 0.1875
- w_key: bfloat16 [1024, 1024], P(None, 'head'), may hold values from -0.1875 to 0.1875
- w_value: bfloat16 [1024, 1024], P(None, 'head'), may hold values from -0.1875 to 0.1875
- w_out: bfloat16 [1024, 1024], P('head'), may hold values from -0.1875 to 0.1875
- temper: float32 [16], P('head'), may hold values from 4 to 12
- adjacency: int32 [128, 128], replicated, may hold values from 0 to 1, as said below
- order: int32 [128], replicated, may hold values from 0 to 127, each once
Outputs:
- update: bfloat16 [16384, 1024], P('ctx', 'head')
The draws below stay inside these ranges and needn't reach their ends.
Inputs may be any that keep to these rules, and one draw needn't show every extreme that they name: Entries are 0 or 1; adjacency[a][a] is 1 for every compartment block a. `order`: each compartment block appears once.
All inputs are finite; a program needn't handle non-finite values.
Results may differ from the reference program's by a relative error of at most 0.015.
Values may be sent and summed in bfloat16 or wider, within the bound.
No kernel may reach another device: no remote copies, remote signals or barrier semaphores. Data moves between devices by JAX's collectives and lax.ppermute only.
A program may use at most 64 MiB of HBM per device.

```python
import math
import jax
import jax.numpy as jnp
from jax import lax

D = 1024
H = 16
HD = 64
BLOCK = 128
TOKENS = 16384
NB = 128


def draw_tokens(key, part):
    first, second, third = jax.random.split(key, 3)
    base = jnp.clip(jax.random.normal(first, (TOKENS, D), jnp.float32), -6.0, 6.0)
    row_scale = jnp.exp(jax.random.uniform(second, (TOKENS, 1), jnp.float32, 0.0, math.log(10.0)))
    col_scale = jnp.exp(jax.random.uniform(third, (1, D), jnp.float32, 0.0, math.log(10.0)))
    return (0.1 * base * row_scale * col_scale).astype(jnp.bfloat16)


def draw_adjacency(key, part):
    first, second = jax.random.split(jax.random.fold_in(key, 7))
    blocks = TOKENS // BLOCK
    reach = jax.random.randint(first, (blocks, 1), 0, blocks // 2 + 1)
    rows = jnp.arange(blocks, dtype=jnp.int32)[:, None]
    cols = jnp.arange(blocks, dtype=jnp.int32)[None, :]
    near = jnp.abs(rows - cols) <= reach
    extra = jax.random.randint(second, (blocks, blocks), 0, 16) == 0
    return (near | extra).astype(jnp.int32)


def steps_of(key, dims, cuts, low, top_value):
    factor_of, own = 1.0, jax.random.fold_in(key, 6)
    for axis_at, shards_of in cuts:
        steps = jnp.exp(jax.random.uniform(jax.random.fold_in(own, axis_at), (shards_of,), jnp.float32, low / len(cuts), top_value / len(cuts)))
        factor_of = factor_of * jnp.repeat(steps, dims[axis_at] // shards_of).reshape([-1 if axis == axis_at else 1 for axis in range(len(dims))])
    return factor_of


def centred(stream_key, extent, spread, most, shards=(), kind=jnp.bfloat16):
    values = jax.random.normal(stream_key, extent, jnp.float32) * spread
    if len(shards) > 0:
        values = steps_of(stream_key, extent, shards, -0.22, 0.18) * values
    return jnp.clip(values, min=-most, max=most).astype(kind)


def setup_inputs(seed: int = 0) -> dict:
    arg_keys = jax.random.split(jax.random.key(seed), 10)
    return {
        "tokens": draw_tokens(jax.random.fold_in(arg_keys[9], 71), 0),
        "gain": jnp.clip(1.0 + 0.15 * jax.random.normal(arg_keys[1], (D,), jnp.float32), 0.25, 1.75),
        "w_query": centred(arg_keys[2], (D, H * HD), D ** -0.5, 0.1875, ((1, 4),)),
        "w_key": centred(arg_keys[3], (D, H * HD), D ** -0.5, 0.1875, ((1, 4),)),
        "w_value": centred(arg_keys[4], (D, H * HD), D ** -0.5, 0.1875, ((1, 4),)),
        "w_out": centred(arg_keys[5], (H * HD, D), (H * HD) ** -0.5, 0.1875, ((0, 4),)),
        "temper": jnp.clip(jnp.exp(math.log(12.0) - 1.0986123 * jax.random.uniform(arg_keys[6], (H,), jnp.float32) ** steps_of(arg_keys[6], (H,), ((0, 4),), -0.2, 0.2)), 4.0, 12.0),
        "adjacency": draw_adjacency(jax.random.fold_in(arg_keys[9], 71), 0),
        "order": jax.random.permutation(arg_keys[8], NB).astype(jnp.int32),
    }


def normalize(values):
    return values * lax.rsqrt(lax.optimization_barrier(jnp.mean(values * values, axis=-1, keepdims=True)) + 1e-06)

def reference(tokens, gain, w_query, w_key, w_value, w_out, temper, adjacency, order):
    total_rows = tokens.shape[0]
    normed = (normalize(tokens.astype(jnp.float32)) * gain).astype(jnp.bfloat16)
    query = normalize(jnp.dot(normed, w_query, preferred_element_type=jnp.float32).reshape(total_rows, H, HD))
    query = (query * (temper[None, :, None] / HD)).astype(jnp.bfloat16)
    keys = normalize(jnp.dot(normed, w_key, preferred_element_type=jnp.float32).reshape(total_rows, H, HD)).astype(jnp.bfloat16)
    values = jnp.dot(normed, w_value, preferred_element_type=jnp.float32).astype(jnp.bfloat16).reshape(total_rows, H, HD)
    linked = adjacency[order][:, order]
    keys_wide = keys.astype(jnp.float32)
    values_wide = values.astype(jnp.float32)

    def one_block(index):
        start = index * BLOCK
        block_query = lax.dynamic_slice_in_dim(query, start, BLOCK, 0).astype(jnp.float32)
        allowed = jnp.repeat(linked[index], BLOCK) > 0
        scores = jnp.einsum('qhd,khd->hqk', block_query, keys_wide)
        probs = jnp.where(allowed[None, None, :], jnp.exp(scores), 0.0)
        weight = lax.optimization_barrier(jnp.sum(probs, axis=-1))
        rounded = lax.optimization_barrier(probs.astype(jnp.bfloat16)).astype(jnp.float32)
        summed = jnp.einsum('hqk,khd->qhd', rounded, values_wide)
        return (summed / weight.T[:, :, None]).astype(jnp.bfloat16)
    attended = lax.map(one_block, jnp.arange(total_rows // BLOCK, dtype=jnp.int32))
    attended = attended.reshape(total_rows, H * HD)
    return jnp.dot(attended, w_out, preferred_element_type=jnp.float32).astype(jnp.bfloat16)
```

```python
import jax
import jax.numpy as jnp
from jax import lax
from jax.experimental import pallas as pl
from jax.experimental.pallas import tpu as pltpu
from jax.sharding import Mesh, PartitionSpec as P

CTX = ("xh", "z", "y")
HEAD = ("xl", "core")
NXH, NZ, NY, NXL, NCORE = 2, 8, 4, 2, 2
SWAP = ("xh", "y", "core")
BLOCK = 128
HD = 64
ROWS = 256
EPS = 1e-06
LOG2E = 1.4426950408889634
DEAD = -30000.0
F32 = jnp.float32
BF16 = jnp.bfloat16
VMEM = pl.BlockSpec(memory_space=pltpu.VMEM)
SMEM = pl.BlockSpec(memory_space=pltpu.SMEM)


def swap_index(xh, y, core):
    return (xh * NY + y) * NCORE + core


def forward_pairs(s):
    return [
        (swap_index(xh, y, k), swap_index(k, (y + s) % NY, xh))
        for xh in range(NXH)
        for y in range(NY)
        for k in range(NCORE)
    ]


def backward_pairs(s):
    return [(b, a) for a, b in forward_pairs(s)]


def project_kernel(y_ref, x_ref, gain_ref, wq_ref, wk_ref, wv_ref, temper_ref, out_ref):
    y = y_ref[0]
    x = x_ref[...].astype(F32)
    scale = lax.rsqrt(jnp.mean(x * x, axis=-1, keepdims=True) + EPS)
    normed = (x * scale * gain_ref[...]).astype(BF16)
    query = jnp.dot(normed, wq_ref[...], preferred_element_type=F32)
    keys = jnp.dot(normed, wk_ref[...], preferred_element_type=F32)
    values = jnp.dot(normed, wv_ref[...], preferred_element_type=F32)

    def unit(part):
        return part * lax.rsqrt(jnp.mean(part * part, axis=-1, keepdims=True) + EPS)

    for j in range(4):
        cols = slice(HD * j, HD * (j + 1))
        q = unit(query[:, cols]) * (temper_ref[0, j] * (LOG2E / HD))
        k = unit(keys[:, cols])
        v = values[:, cols]
        slot = lax.rem(j - y + NY, NY)
        out_ref[slot, :ROWS, :] = jnp.concatenate([k, v], axis=1).astype(BF16)
        out_ref[slot, ROWS:, :] = jnp.concatenate([q[:BLOCK], q[BLOCK:]], axis=1).astype(BF16)


def project(y, whole, gain, w_query, w_key, w_value, temper):
    return pl.pallas_call(
        project_kernel,
        out_shape=jax.ShapeDtypeStruct((4, ROWS + BLOCK, 128), BF16),
        in_specs=[SMEM, VMEM, VMEM, VMEM, VMEM, VMEM, SMEM],
        out_specs=VMEM,
        compiler_params=pltpu.CompilerParams(vmem_limit_bytes=32 << 20),
        name="project",
    )(y, whole, gain, w_query, w_key, w_value, temper)


QT = 256
KT = 512
NQ = 2048
NK = 1024


def widen_kernel(mine_ref, other_ref, out_ref):
    lane = lax.broadcasted_iota(jnp.int32, (BLOCK, 128), 1)
    for m in range(8):
        pair = (mine_ref if m < 4 else other_ref)[m % 4].astype(F32)
        for b in range(2):
            part = pair if b == 0 else pltpu.roll(pair, 64, 1)
            flag = jnp.where(lane == HD + 2 * m + b, 1.0, 0.0)
            at = (2 * m + b) * BLOCK
            out_ref[at : at + BLOCK, :] = jnp.where(lane < HD, part, flag).astype(BF16)


def widen(mine, other):
    return pl.pallas_call(
        widen_kernel,
        out_shape=jax.ShapeDtypeStruct((NQ, 128), BF16),
        in_specs=[VMEM, VMEM],
        out_specs=VMEM,
        name="widen",
    )(mine, other)


def attend_kernel(first, pieces, where_ref, q_ref, bias_ref, *refs):
    kv_refs, acc_ref = refs[: len(pieces)], refs[-1]
    lane = lax.broadcasted_iota(jnp.int32, (KT, 128), 1)
    if first:
        acc_ref[...] = jnp.zeros_like(acc_ref)

    for n, (slot, offset) in enumerate(pieces):

        def tile(c, carry):
            kv = kv_refs[n][pl.ds(pl.multiple_of(c * KT, KT), KT), :].astype(F32)
            at = offset // BLOCK + c * (KT // BLOCK)
            chunk = where_ref[slot]
            bias = jnp.concatenate(
                [
                    jnp.broadcast_to(bias_ref[chunk, pl.ds(at + b, 1), :], (BLOCK, 128))
                    for b in range(KT // BLOCK)
                ],
                axis=0,
            )
            kx = jnp.where(lane < HD, kv, bias).astype(BF16)
            vx = jnp.where(lane < HD, 1.0, kv).astype(BF16)
            for t in range(NQ // QT):
                rows = slice(t * QT, (t + 1) * QT)
                scores = lax.dot_general(
                    q_ref[rows, :], kx, (((1,), (1,)), ((), ())), preferred_element_type=F32
                )
                probs = jnp.exp2(scores).astype(BF16)
                acc_ref[rows, :] += jnp.dot(probs, vx, preferred_element_type=F32)
            return carry

        lax.fori_loop(0, kv_refs[n].shape[0] // KT, tile, 0)


def attend(where, q, bias, kvs, acc):
    first = acc is None
    pieces = tuple((slot, offset) for _, slot, offset in kvs)
    operands = [where, q, bias] + [kv for kv, _, _ in kvs] + ([] if first else [acc])
    body = lambda *refs: attend_kernel(first, pieces, *refs)
    return pl.pallas_call(
        body,
        out_shape=jax.ShapeDtypeStruct((NQ, 128), F32),
        in_specs=[SMEM] + [VMEM] * (len(operands) - 1),
        out_specs=VMEM,
        input_output_aliases={} if first else {len(operands) - 1: 0},
        compiler_params=pltpu.CompilerParams(vmem_limit_bytes=32 << 20),
        cost_estimate=pl.CostEstimate(
            flops=512 * NQ * sum(kv.shape[0] for kv, _, _ in kvs),
            transcendentals=NQ * sum(kv.shape[0] for kv, _, _ in kvs),
            bytes_accessed=4 << 20,
        ),
        name="attend",
    )(*operands)


def finish_kernel(mine_ref, other_ref, out_ref):
    total = mine_ref[...] + other_ref[...]
    ratio = total / pltpu.roll(total, 64, 1)
    lane = lax.broadcasted_iota(jnp.int32, (BLOCK, 128), 1)
    for m in range(4):
        first = pltpu.roll(ratio[2 * m * BLOCK : (2 * m + 1) * BLOCK], 64, 1)
        second = ratio[(2 * m + 1) * BLOCK : (2 * m + 2) * BLOCK]
        out_ref[m] = jnp.where(lane < HD, first, second).astype(BF16)


def finish(mine, other):
    return pl.pallas_call(
        finish_kernel,
        out_shape=jax.ShapeDtypeStruct((4, BLOCK, 128), BF16),
        in_specs=[VMEM, VMEM],
        out_specs=VMEM,
        name="finish",
    )(mine, other)


def output_kernel(y_ref, a_ref, w_ref, out_ref):
    y = y_ref[0]
    lane = lax.broadcasted_iota(jnp.int32, (BLOCK, 128), 1)
    lefts, rights, weights = [], [], []
    for source in range(4):
        for s in range(4):
            pair = a_ref[4 * source + s].astype(F32)
            lefts.append(jnp.where(lane < HD, pair, 0.0).astype(BF16))
            rights.append(jnp.where(lane < HD, 0.0, pair).astype(BF16))
            j = lax.rem(y + s, NY)
            row = pl.multiple_of(source * 256 + j * HD, HD)
            w = w_ref[pl.ds(row, HD), :]
            weights += [w, w]
    w = jnp.concatenate(weights, axis=0)
    out_ref[:BLOCK, :] = jnp.dot(jnp.concatenate(lefts, axis=1), w, preferred_element_type=F32).astype(BF16)
    out_ref[BLOCK:, :] = jnp.dot(jnp.concatenate(rights, axis=1), w, preferred_element_type=F32).astype(BF16)


def output(y, attended, w):
    return pl.pallas_call(
        output_kernel,
        out_shape=jax.ShapeDtypeStruct((ROWS, 256), BF16),
        in_specs=[SMEM, VMEM, VMEM],
        out_specs=VMEM,
        compiler_params=pltpu.CompilerParams(vmem_limit_bytes=32 << 20),
        name="output",
    )(y, attended, w)


def columns(w_out):
    me = lax.axis_index(HEAD)
    pieces = [lax.dynamic_slice_in_dim(w_out, me * 256, 256, 1)]
    for d in (1, 2, 3):
        block = lax.dynamic_slice_in_dim(w_out, ((me + d) % 4) * 256, 256, 1)
        pieces.append(lax.ppermute(block, HEAD, [(i, (i + d) % 4) for i in range(4)]))
    whole = jnp.zeros((1024, 256), w_out.dtype)
    for d in range(4):
        whole = lax.dynamic_update_slice_in_dim(whole, pieces[d], ((me - d) % 4) * 256, 0)
    return whole


def bias_table(adjacency, order):
    core, y, z = lax.axis_index("core"), lax.axis_index("y"), lax.axis_index("z")
    spin = (y - jnp.arange(NY, dtype=jnp.int32)) % NY
    two = jnp.arange(2, dtype=jnp.int32)
    block = lambda xh, zs: 2 * ((xh * NZ + zs[:, None, None]) * NY + spin[None, :, None]) + two[None, None, :]
    keys = block(core, jnp.arange(NZ, dtype=jnp.int32)).reshape(-1)
    queries = jnp.concatenate([block(core, z[None]).reshape(-1), block(1 - core, z[None]).reshape(-1)])
    ids = jnp.arange(128, dtype=jnp.int32)
    pick = lambda at: (order[at][:, None] == ids[None, :]).astype(BF16)
    picked = jnp.dot(pick(queries), adjacency.astype(BF16), preferred_element_type=F32).astype(BF16)
    live = jnp.dot(pick(keys), picked.T, preferred_element_type=F32)
    bias = jnp.where(live > 0.5, 0.0, DEAD)
    return jnp.pad(bias, ((0, 0), (64, 48))).reshape(NZ, NK // BLOCK, 128)


def shards(tokens, gain, w_query, w_key, w_value, w_out, temper, adjacency, order):
    y = lax.axis_index("y").astype(jnp.int32)[None]
    whole = lax.all_gather(tokens, HEAD, axis=1, tiled=True)
    messages = project(y, whole, gain[None, :], w_query, w_key, w_value, temper[None, :])
    got = [lax.ppermute(messages[s], SWAP, forward_pairs(s)) for s in range(NY)]
    got = jnp.stack(got)
    kv = got[:, :ROWS, :].reshape(4 * ROWS, 128)
    query = got[:, ROWS:, :]
    up = [(i, (i + 1) % NZ) for i in range(NZ)]
    down = [(i, (i - 1) % NZ) for i in range(NZ)]
    z = lax.axis_index("z").astype(jnp.int32)
    where = (z + jnp.array([0, -1, 1, -2, 2, -3, 3, 4], jnp.int32)) % NZ
    lower, upper = [kv], [kv]
    query_other = lax.ppermute(query, "core", [(0, 1), (1, 0)])
    lower.append(lax.ppermute(kv, "z", up))
    upper.append(lax.ppermute(kv, "z", down))
    w_columns = columns(w_out)
    bias = bias_table(adjacency, order)
    q = widen(query, query_other)
    acc = attend(where, q, bias, [(kv, 0, 0)], None)
    for d in (1, 2, 3):
        low, high, acc = lax.optimization_barrier((lower[d], upper[d], acc))
        if d < 3:
            lower.append(lax.ppermute(low, "z", up))
            upper.append(lax.ppermute(high, "z", down))
        else:
            far_low = lax.ppermute(low[: NK // 2], "z", up)
            far_high = lax.ppermute(high[NK // 2 :], "z", down)
        acc = attend(where, q, bias, [(low, 2 * d - 1, 0), (high, 2 * d, 0)], acc)
        if d == 2:
            acc, w_columns = lax.optimization_barrier((acc, w_columns))
    acc = attend(where, q, bias, [(far_low, 7, 0), (far_high, 7, NK // 2)], acc)
    other = lax.ppermute(acc[NQ // 2 :], "core", [(0, 1), (1, 0)])
    attended = finish(acc[: NQ // 2], other)
    back = jnp.stack([lax.ppermute(attended[s], SWAP, backward_pairs(s)) for s in range(NY)])
    gathered = lax.all_gather(back, HEAD, axis=0, tiled=True)
    return output(y, gathered, w_columns)


def solution(mesh):
    fine = Mesh(mesh.devices.reshape(NXH, NZ, NY, NXL, NCORE), CTX + HEAD)
    in_specs = (
        P(CTX, HEAD),
        P(),
        P(None, HEAD),
        P(None, HEAD),
        P(None, HEAD),
        P(HEAD, None),
        P(HEAD),
        P(),
        P(),
    )
    return jax.shard_map(shards, mesh=fine, in_specs=in_specs, out_specs=P(CTX, HEAD), check_vma=False)
```

```python
import jax
import jax.numpy as jnp
from jax import lax
from jax.experimental import pallas as pl
from jax.experimental.pallas import tpu as pltpu
from jax.sharding import Mesh, PartitionSpec as P

CTX = ("xh", "z", "y")
HEAD = ("xl", "core")
NXH, NZ, NY, NXL, NCORE = 2, 8, 4, 2, 2
BLOCK = 128
HD = 64
ROWS = 256
EPS = 1e-06
LOG2E = 1.4426950408889634
DEAD = -30000.0
F32 = jnp.float32
BF16 = jnp.bfloat16
VMEM = pl.BlockSpec(memory_space=pltpu.VMEM)
SMEM = pl.BlockSpec(memory_space=pltpu.SMEM)
HBM = pl.BlockSpec(memory_space=pltpu.HBM)
PARAMS = pltpu.CompilerParams(vmem_limit_bytes=32 << 20)


def ring(length, by):
    return [(i, (i + by) % length) for i in range(length)]


def project_kernel(
    temper_ref, x_ref, gain_hbm, wq_hbm, wk_hbm, wv_hbm, *refs
):
    out_refs, (stage_ref, gain_ref, wq_ref, wk_ref, wv_ref, sems) = refs[:NY], refs[NY:]
    pairs = ((gain_hbm, gain_ref), (wq_hbm, wq_ref), (wk_hbm, wk_ref), (wv_hbm, wv_ref))
    copies = [pltpu.make_async_copy(source, target, sems.at[n]) for n, (source, target) in enumerate(pairs)]
    for copy in copies:
        copy.start()
    x = x_ref[...].astype(F32)
    scaled = x * lax.rsqrt(jnp.mean(x * x, axis=-1, keepdims=True) + EPS)
    copies[0].wait()
    normed = (scaled * gain_ref[...]).astype(BF16)
    copies[1].wait()
    query = jnp.dot(normed, wq_ref[...], preferred_element_type=F32)
    copies[2].wait()
    keys = jnp.dot(normed, wk_ref[...], preferred_element_type=F32)
    copies[3].wait()
    values = jnp.dot(normed, wv_ref[...], preferred_element_type=F32)

    def unit(part):
        return part * lax.rsqrt(jnp.mean(part * part, axis=-1, keepdims=True) + EPS)

    for j in range(4):
        cols = slice(HD * j, HD * (j + 1))
        q = unit(query[:, cols]) * (temper_ref[j] * (LOG2E / HD))
        k = unit(keys[:, cols])
        v = values[:, cols]
        stage_ref[j, :ROWS, :] = jnp.concatenate([k, v], axis=1).astype(BF16)
        stage_ref[j, ROWS:, :] = jnp.concatenate([q[:BLOCK], q[BLOCK:]], axis=1).astype(BF16)
    y = lax.axis_index("y").astype(jnp.int32)
    for s in range(NY):
        out_refs[s][...] = stage_ref[lax.rem(y + s, NY)]


def project(whole, gain, w_query, w_key, w_value, temper):
    hold = lambda x: pltpu.with_memory_space_constraint(x, pltpu.HBM)
    return pl.pallas_call(
        project_kernel,
        out_shape=[jax.ShapeDtypeStruct((ROWS + BLOCK, 128), BF16)] * NY,
        in_specs=[SMEM, VMEM, HBM, HBM, HBM, HBM],
        out_specs=[VMEM] * NY,
        scratch_shapes=[
            pltpu.VMEM((NY, ROWS + BLOCK, 128), BF16),
            pltpu.VMEM((1, 1024), F32),
            pltpu.VMEM((1024, 256), BF16),
            pltpu.VMEM((1024, 256), BF16),
            pltpu.VMEM((1024, 256), BF16),
            pltpu.SemaphoreType.DMA((4,)),
        ],
        compiler_params=PARAMS,
        name="project",
    )(temper, whole, hold(gain), hold(w_query), hold(w_key), hold(w_value))


QT = 256
NQ = 1024
NK = 1024


def widen(packed_ref, first, out_ref):
    lane = lax.broadcasted_iota(jnp.int32, (BLOCK, 128), 1)
    for m in range(NY):
        pair = packed_ref[m].astype(F32)
        for b in range(2):
            part = pair if b == 0 else pltpu.roll(pair, 64, 1)
            flag = jnp.where(lane == HD + first + 2 * m + b, 1.0, 0.0)
            at = (2 * m + b) * BLOCK
            out_ref[at : at + BLOCK, :] = jnp.where(lane < HD, part, flag).astype(BF16)


def bias_rows(order_ref, adjacency_ref, keys_ref, queries_ref, bias_ref):
    z, y, xh = (lax.axis_index(a).astype(jnp.int32) for a in ("z", "y", "xh"))
    lane = lax.broadcasted_iota(jnp.int32, (1, 128), 1)

    def pick(side, zs, s, b):
        block = 2 * ((side * NZ + zs) * NY + lax.rem(y - s + NY, NY)) + b
        return jnp.where(lane == order_ref[block], 1.0, 0.0)

    queries_ref[...] = jnp.zeros_like(queries_ref)
    for s in range(NY):
        for b in range(2):
            n = 2 * s + b
            queries_ref[HD + n : HD + n + 1, :] = pick(xh, z, s, b)
            queries_ref[HD + 8 + n : HD + 9 + n, :] = pick(1 - xh, z, s, b)
            for zs in range(NZ):
                keys_ref[8 * zs + n : 8 * zs + n + 1, :] = pick(xh, zs, s, b)
    turned = (((1,), (1,)), ((), ()))
    adjacency = adjacency_ref[...].astype(F32).astype(BF16)
    keys, queries = keys_ref[...].astype(BF16), queries_ref[...].astype(BF16)
    picked = lax.dot_general(keys, adjacency, turned, preferred_element_type=F32).astype(BF16)
    live = lax.dot_general(picked, queries, turned, preferred_element_type=F32)
    bias_ref[...] = jnp.where(live > 0.5, 0.0, DEAD).reshape(NZ, NK // BLOCK, 128)


def chunk_at(distance):
    return lax.rem(lax.axis_index("z").astype(jnp.int32) + (distance + NZ), NZ)


def split_kv(kv, distance, bias_ref):
    lane = lax.broadcasted_iota(jnp.int32, (NK, 128), 1)
    kv = kv.astype(F32)
    table = bias_ref[chunk_at(distance)]
    bias = jnp.concatenate(
        [jnp.broadcast_to(table[b : b + 1, :], (BLOCK, 128)) for b in range(NK // BLOCK)], axis=0
    )
    return jnp.where(lane < HD, kv, bias).astype(BF16), jnp.where(lane < HD, 1.0, kv).astype(BF16)


def tile(q_ref, kx, vx, store):
    for t in range(NQ // QT):
        rows = slice(t * QT, (t + 1) * QT)
        scores = lax.dot_general(q_ref[rows, :], kx, (((1,), (1,)), ((), ())), preferred_element_type=F32)
        probs = jnp.exp2(scores).astype(BF16)
        store(rows, jnp.dot(probs, vx, preferred_element_type=F32))


def put(ref):
    def store(rows, part):
        ref[rows, :] = part

    return store


def add(ref):
    def store(rows, part):
        ref[rows, :] += part

    return store


def cost(keys):
    return pl.CostEstimate(flops=512 * NQ * keys, transcendentals=NQ * keys, bytes_accessed=4 << 20)


ACC = jax.ShapeDtypeStruct((NQ, 128), F32)
WIDE = jax.ShapeDtypeStruct((NQ, 128), BF16)


def first_kernel(order_ref, adjacency_ref, mine_ref, kv_ref, q_ref, bias_ref, acc_ref, keys_ref, queries_ref):
    bias_rows(order_ref, adjacency_ref, keys_ref, queries_ref, bias_ref)
    widen(mine_ref, 0, q_ref)
    kx, vx = split_kv(kv_ref[...], 0, bias_ref)
    tile(q_ref, kx, vx, put(acc_ref))


def attend_first(order, adjacency, mine, kv):
    return pl.pallas_call(
        first_kernel,
        out_shape=(WIDE, jax.ShapeDtypeStruct((NZ, NK // BLOCK, 128), F32), ACC),
        in_specs=[SMEM, VMEM, VMEM, VMEM],
        out_specs=(VMEM, VMEM, VMEM),
        scratch_shapes=[pltpu.VMEM((64, 128), F32), pltpu.VMEM((128, 128), F32)],
        compiler_params=PARAMS,
        cost_estimate=cost(NK),
        name="attend_first",
    )(order, adjacency, mine, kv)


def both_tiles(step, bias_ref, low_ref, high_ref, kx_ref, vx_ref, pairs):
    kx_ref[0], vx_ref[0] = split_kv(low_ref[...], -step, bias_ref)
    kx_ref[1], vx_ref[1] = split_kv(high_ref[...], step, bias_ref)

    def body(n, carry):
        kx, vx = kx_ref[n], vx_ref[n]
        for q_ref, acc_ref in pairs:
            tile(q_ref, kx, vx, add(acc_ref))
        return carry

    lax.fori_loop(0, 2, body, 0)


SPLIT = [pltpu.VMEM((2, NK, 128), BF16), pltpu.VMEM((2, NK, 128), BF16)]


def second_kernel(
    q_ref, other_ref, bias_ref, kv_ref, low_ref, high_ref, acc_in, q2_ref, acc_ref, acc2_ref, kx_ref, vx_ref
):
    widen(other_ref, 8, q2_ref)
    kx, vx = split_kv(kv_ref[...], 0, bias_ref)
    tile(q2_ref, kx, vx, put(acc2_ref))
    both_tiles(1, bias_ref, low_ref, high_ref, kx_ref, vx_ref, ((q_ref, acc_ref), (q2_ref, acc2_ref)))


def attend_second(q, other, bias, kv, low, high, acc):
    return pl.pallas_call(
        second_kernel,
        out_shape=(WIDE, ACC, ACC),
        in_specs=[VMEM] * 7,
        out_specs=(VMEM, VMEM, VMEM),
        scratch_shapes=SPLIT,
        input_output_aliases={6: 1},
        compiler_params=PARAMS,
        cost_estimate=cost(5 * NK),
        name="attend_second",
    )(q, other, bias, kv, low, high, acc)


def middle_kernel(step, q_ref, q2_ref, bias_ref, low_ref, high_ref, in1, in2, acc_ref, acc2_ref, kx_ref, vx_ref):
    both_tiles(step, bias_ref, low_ref, high_ref, kx_ref, vx_ref, ((q_ref, acc_ref), (q2_ref, acc2_ref)))


def attend_middle(step, q, q2, bias, low, high, acc, acc2):
    return pl.pallas_call(
        lambda *refs: middle_kernel(step, *refs),
        out_shape=(ACC, ACC),
        in_specs=[VMEM] * 7,
        out_specs=(VMEM, VMEM),
        scratch_shapes=SPLIT,
        input_output_aliases={5: 0, 6: 1},
        compiler_params=PARAMS,
        cost_estimate=cost(4 * NK),
        name="attend_middle",
    )(q, q2, bias, low, high, acc, acc2)


HALF = NQ // 2
SUMS = 16


def split_last(low_ref, high_ref, bias_ref):
    return split_kv(jnp.concatenate([low_ref[...], high_ref[...]], axis=0), NZ // 2, bias_ref)


def last_other_kernel(q_ref, bias_ref, low_ref, high_ref, in_ref, message_ref, acc_ref):
    def store(rows, part):
        acc_ref[rows, :] = in_ref[rows, :] + part

    tile(q_ref, *split_last(low_ref, high_ref, bias_ref), store)
    lane = lax.broadcasted_iota(jnp.int32, (BLOCK, 128), 1)
    row = lax.broadcasted_iota(jnp.int32, (SUMS, 128), 0)
    column = lax.broadcasted_iota(jnp.int32, (SUMS, 128), 1)
    sums = jnp.zeros((SUMS, BLOCK), F32)
    blocks = [acc_ref[n * BLOCK : (n + 1) * BLOCK, :] for n in range(8)]
    for m in range(NY):
        pair = jnp.where(lane < HD, pltpu.roll(blocks[2 * m], 64, 1), blocks[2 * m + 1])
        message_ref[m * BLOCK : (m + 1) * BLOCK, :] = pair.astype(BF16)
    for n in range(8):
        coarse = blocks[n].astype(BF16).astype(F32)
        spread = jnp.where(lane == 0, coarse, jnp.where(lane == 1, blocks[n] - coarse, 0.0)).astype(BF16)
        at = jnp.where((row // 2 == n) & (row % 2 == column), 1.0, 0.0).astype(BF16)
        sums += lax.dot_general(at, spread, (((1,), (1,)), ((), ())), preferred_element_type=F32)
    message_ref[HALF:, :] = sums.astype(BF16)


def attend_last_other(q2, bias, low, high, acc2):
    return pl.pallas_call(
        last_other_kernel,
        out_shape=jax.ShapeDtypeStruct((HALF + SUMS, 128), BF16),
        in_specs=[VMEM] * 5,
        out_specs=VMEM,
        scratch_shapes=[pltpu.VMEM((NQ, 128), F32)],
        compiler_params=PARAMS,
        cost_estimate=cost(NK),
        name="attend_last_other",
    )(q2, bias, low, high, acc2)


def last_mine_kernel(q_ref, bias_ref, low_ref, high_ref, in_ref, acc_ref):
    tile(q_ref, *split_last(low_ref, high_ref, bias_ref), add(acc_ref))


def attend_last_mine(q, bias, low, high, acc):
    return pl.pallas_call(
        last_mine_kernel,
        out_shape=ACC,
        in_specs=[VMEM] * 5,
        out_specs=VMEM,
        input_output_aliases={4: 0},
        compiler_params=PARAMS,
        cost_estimate=cost(NK),
        name="attend_last_mine",
    )(q, bias, low, high, acc)


def finish_kernel(mine_ref, message_ref, *out_refs):
    lane = lax.broadcasted_iota(jnp.int32, (BLOCK, 128), 1)
    row = lax.broadcasted_iota(jnp.int32, (SUMS, 128), 0)
    sums = message_ref[HALF:, :]
    blocks = [mine_ref[n * BLOCK : (n + 1) * BLOCK, :] for n in range(8)]
    spread = []
    for n in range(8):
        at = jnp.where(row // 2 == n, 1.0, 0.0).astype(BF16)
        spread.append(lax.dot_general(sums, at, (((0,), (0,)), ((), ())), preferred_element_type=F32))
    for m in range(NY):
        one, two = blocks[2 * m], blocks[2 * m + 1]
        total = jnp.where(lane < HD, pltpu.roll(one, 64, 1), two)
        total += message_ref[m * BLOCK : (m + 1) * BLOCK, :].astype(F32)
        weight = jnp.where(lane < HD, one + spread[2 * m], pltpu.roll(two, 64, 1) + spread[2 * m + 1])
        out_refs[m][...] = (total / weight).astype(BF16)


def finish(mine, message):
    return pl.pallas_call(
        finish_kernel,
        out_shape=[jax.ShapeDtypeStruct((BLOCK, 128), BF16)] * NY,
        in_specs=[VMEM, VMEM],
        out_specs=[VMEM] * NY,
        compiler_params=PARAMS,
        name="finish",
    )(mine, message)


def output_kernel(a_ref, w_ref, out_ref):
    y = lax.axis_index("y").astype(jnp.int32)
    lane = lax.broadcasted_iota(jnp.int32, (BLOCK, 128), 1)
    lefts, rights, weights = [], [], []
    for source in range(4):
        for s in range(4):
            pair = a_ref[4 * source + s].astype(F32)
            lefts.append(jnp.where(lane < HD, pair, 0.0).astype(BF16))
            rights.append(jnp.where(lane < HD, 0.0, pair).astype(BF16))
            j = lax.rem(y + s, NY)
            row = pl.multiple_of(source * 256 + j * HD, HD)
            w = w_ref[pl.ds(row, HD), :]
            weights += [w, w]
    w = jnp.concatenate(weights, axis=0)
    out_ref[:BLOCK, :] = jnp.dot(jnp.concatenate(lefts, axis=1), w, preferred_element_type=F32).astype(BF16)
    out_ref[BLOCK:, :] = jnp.dot(jnp.concatenate(rights, axis=1), w, preferred_element_type=F32).astype(BF16)


def output(attended, w):
    return pl.pallas_call(
        output_kernel,
        out_shape=jax.ShapeDtypeStruct((ROWS, 256), BF16),
        in_specs=[VMEM, VMEM],
        out_specs=VMEM,
        compiler_params=PARAMS,
        name="output",
    )(attended, w)


def shards(tokens, gain, w_query, w_key, w_value, w_out, temper, adjacency, order):
    whole = lax.all_gather(tokens, HEAD, axis=1, tiled=True)
    messages = project(whole, gain[None, :], w_query, w_key, w_value, temper)
    got = jnp.stack([messages[0]] + [lax.ppermute(messages[s], "y", ring(NY, s)) for s in range(1, NY)])
    kv = got[:, :ROWS, :].reshape(NK, 128)
    query = got[:, ROWS:, :]
    query, kv = lax.optimization_barrier((query, kv))
    low, high = lax.ppermute(kv, "z", ring(NZ, 1)), lax.ppermute(kv, "z", ring(NZ, -1))
    other = lax.ppermute(query, "xh", [(0, 1), (1, 0)])
    q, bias, acc = attend_first(order, adjacency, query, kv)
    w_late, _ = lax.optimization_barrier((w_out, kv))
    w_whole = lax.all_gather(w_late, HEAD, axis=0, tiled=True)
    for step in (1, 2, 3):
        low, high, acc = lax.optimization_barrier((low, high, acc))
        if step < 3:
            next_low, next_high = lax.ppermute(low, "z", ring(NZ, 1)), lax.ppermute(high, "z", ring(NZ, -1))
        else:
            next_low = lax.ppermute(low[: NK // 2], "z", ring(NZ, 1))
            next_high = lax.ppermute(high[NK // 2 :], "z", ring(NZ, -1))
        if step == 1:
            q2, acc, acc2 = attend_second(q, other, bias, kv, low, high, acc)
        else:
            acc, acc2 = attend_middle(step, q, q2, bias, low, high, acc, acc2)
        low, high = next_low, next_high
    low, high, acc, w_whole = lax.optimization_barrier((low, high, acc, w_whole))
    w_columns = lax.dynamic_slice_in_dim(w_whole, lax.axis_index(HEAD) * 256, 256, 1)
    message = attend_last_other(q2, bias, low, high, acc2)
    message, acc = lax.optimization_barrier((message, acc))
    message = lax.ppermute(message, "xh", [(0, 1), (1, 0)])
    attended = finish(attend_last_mine(q, bias, low, high, acc), message)
    back = jnp.stack([attended[0]] + [lax.ppermute(attended[s], "y", ring(NY, -s)) for s in range(1, NY)])
    gathered = lax.all_gather(back, HEAD, axis=0, tiled=True)
    return output(gathered, w_columns)


def solution(mesh):
    fine = Mesh(mesh.devices.reshape(NXH, NZ, NY, NXL, NCORE), CTX + HEAD)
    in_specs = (
        P(CTX, HEAD),
        P(),
        P(None, HEAD),
        P(None, HEAD),
        P(None, HEAD),
        P(HEAD, None),
        P(HEAD),
        P(),
        P(),
    )
    return jax.shard_map(shards, mesh=fine, in_specs=in_specs, out_specs=P(CTX, HEAD), check_vma=False)
```

```python
import jax
import jax.numpy as jnp
from jax import lax
from jax.experimental import pallas as pl
from jax.experimental.pallas import tpu as pltpu
from jax.sharding import Mesh, PartitionSpec as P

CTX = ("xh", "z", "y")
HEAD = ("xl", "core")
NXH, NZ, NY, NXL, NCORE = 2, 8, 4, 2, 2
BLOCK = 128
HD = 64
ROWS = 256
EPS = 1e-06
LOG2E = 1.4426950408889634
DEAD = -30000.0
F32 = jnp.float32
BF16 = jnp.bfloat16
VMEM = pl.BlockSpec(memory_space=pltpu.VMEM)
SMEM = pl.BlockSpec(memory_space=pltpu.SMEM)
HBM = pl.BlockSpec(memory_space=pltpu.HBM)
PARAMS = pltpu.CompilerParams(vmem_limit_bytes=32 << 20)


def ring(length, by):
    return [(i, (i + by) % length) for i in range(length)]


def project_kernel(
    x_ref, temper_hbm, gain_hbm, wq_hbm, wk_hbm, wv_hbm, *refs
):
    out_refs, (stage_ref, temper_ref, gain_ref, wq_ref, wk_ref, wv_ref, sems) = refs[:NY], refs[NY:]
    pairs = (
        (gain_hbm, gain_ref),
        (wq_hbm, wq_ref),
        (wk_hbm, wk_ref),
        (wv_hbm, wv_ref),
        (temper_hbm, temper_ref),
    )
    copies = [pltpu.make_async_copy(source, target, sems.at[n]) for n, (source, target) in enumerate(pairs)]
    for copy in copies:
        copy.start()
    x = x_ref[...].astype(F32)
    scaled = x * lax.rsqrt(jnp.mean(x * x, axis=-1, keepdims=True) + EPS)
    copies[0].wait()
    normed = (scaled * gain_ref[...]).astype(BF16)
    copies[1].wait()
    query = jnp.dot(normed, wq_ref[...], preferred_element_type=F32)
    copies[2].wait()
    keys = jnp.dot(normed, wk_ref[...], preferred_element_type=F32)
    copies[3].wait()
    values = jnp.dot(normed, wv_ref[...], preferred_element_type=F32)

    copies[4].wait()

    def unit(part):
        return part * lax.rsqrt(jnp.mean(part * part, axis=-1, keepdims=True) + EPS)

    for j in range(4):
        cols = slice(HD * j, HD * (j + 1))
        q = unit(query[:, cols]) * (temper_ref[j] * (LOG2E / HD))
        k = unit(keys[:, cols])
        v = values[:, cols]
        stage_ref[j, :ROWS, :] = jnp.concatenate([k, v], axis=1).astype(BF16)
        stage_ref[j, ROWS:, :] = jnp.concatenate([q[:BLOCK], q[BLOCK:]], axis=1).astype(BF16)
    y = lax.axis_index("y").astype(jnp.int32)
    for s in range(NY):
        out_refs[s][...] = stage_ref[lax.rem(y + s, NY)]


def project(whole, gain, w_query, w_key, w_value, temper):
    hold = lambda x: pltpu.with_memory_space_constraint(x, pltpu.HBM)
    return pl.pallas_call(
        project_kernel,
        out_shape=[jax.ShapeDtypeStruct((ROWS + BLOCK, 128), BF16)] * NY,
        in_specs=[VMEM, HBM, HBM, HBM, HBM, HBM],
        out_specs=[VMEM] * NY,
        scratch_shapes=[
            pltpu.VMEM((NY, ROWS + BLOCK, 128), BF16),
            pltpu.SMEM((4,), F32),
            pltpu.VMEM((1, 1024), F32),
            pltpu.VMEM((1024, 256), BF16),
            pltpu.VMEM((1024, 256), BF16),
            pltpu.VMEM((1024, 256), BF16),
            pltpu.SemaphoreType.DMA((5,)),
        ],
        compiler_params=PARAMS,
        name="project",
    )(whole, hold(temper), hold(gain), hold(w_query), hold(w_key), hold(w_value))


QT = 256
NQ = 1024
NK = 1024


def widen(packed_ref, first, out_ref):
    lane = lax.broadcasted_iota(jnp.int32, (BLOCK, 128), 1)
    for m in range(NY):
        pair = packed_ref[m].astype(F32)
        for b in range(2):
            part = pair if b == 0 else pltpu.roll(pair, 64, 1)
            flag = jnp.where(lane == HD + first + 2 * m + b, 1.0, 0.0)
            at = (2 * m + b) * BLOCK
            out_ref[at : at + BLOCK, :] = jnp.where(lane < HD, part, flag).astype(BF16)


def bias_rows(order_ref, adjacency_ref, keys_ref, queries_ref, bias_ref):
    z, y, xh = (lax.axis_index(a).astype(jnp.int32) for a in ("z", "y", "xh"))
    lane = lax.broadcasted_iota(jnp.int32, (1, 128), 1)

    def pick(side, zs, s, b):
        block = 2 * ((side * NZ + zs) * NY + lax.rem(y - s + NY, NY)) + b
        return jnp.where(lane == order_ref[block], 1.0, 0.0)

    queries_ref[...] = jnp.zeros_like(queries_ref)
    for s in range(NY):
        for b in range(2):
            n = 2 * s + b
            queries_ref[HD + n : HD + n + 1, :] = pick(xh, z, s, b)
            queries_ref[HD + 8 + n : HD + 9 + n, :] = pick(1 - xh, z, s, b)
            for zs in range(NZ):
                keys_ref[8 * zs + n : 8 * zs + n + 1, :] = pick(xh, zs, s, b)
    turned = (((1,), (1,)), ((), ()))
    adjacency = adjacency_ref[...].astype(F32).astype(BF16)
    keys, queries = keys_ref[...].astype(BF16), queries_ref[...].astype(BF16)
    picked = lax.dot_general(keys, adjacency, turned, preferred_element_type=F32).astype(BF16)
    live = lax.dot_general(picked, queries, turned, preferred_element_type=F32)
    bias_ref[...] = jnp.where(live > 0.5, 0.0, DEAD).reshape(NZ, NK // BLOCK, 128)


def chunk_at(distance):
    return lax.rem(lax.axis_index("z").astype(jnp.int32) + (distance + NZ), NZ)


def split_kv(kv, distance, bias_ref):
    lane = lax.broadcasted_iota(jnp.int32, (NK, 128), 1)
    kv = kv.astype(F32)
    table = bias_ref[chunk_at(distance)]
    bias = jnp.concatenate(
        [jnp.broadcast_to(table[b : b + 1, :], (BLOCK, 128)) for b in range(NK // BLOCK)], axis=0
    )
    return jnp.where(lane < HD, kv, bias).astype(BF16), jnp.where(lane < HD, 1.0, kv).astype(BF16)


def tile(q_ref, kx, vx, store):
    for t in range(NQ // QT):
        rows = slice(t * QT, (t + 1) * QT)
        scores = lax.dot_general(q_ref[rows, :], kx, (((1,), (1,)), ((), ())), preferred_element_type=F32)
        probs = jnp.exp2(scores).astype(BF16)
        store(rows, jnp.dot(probs, vx, preferred_element_type=F32))


def put(ref):
    def store(rows, part):
        ref[rows, :] = part

    return store


def add(ref):
    def store(rows, part):
        ref[rows, :] += part

    return store


def cost(keys):
    return pl.CostEstimate(flops=512 * NQ * keys, transcendentals=NQ * keys, bytes_accessed=4 << 20)


ACC = jax.ShapeDtypeStruct((NQ, 128), F32)
WIDE = jax.ShapeDtypeStruct((NQ, 128), BF16)


def first_kernel(order_ref, adjacency_ref, mine_ref, kv_ref, q_ref, bias_ref, acc_ref, keys_ref, queries_ref):
    bias_rows(order_ref, adjacency_ref, keys_ref, queries_ref, bias_ref)
    widen(mine_ref, 0, q_ref)
    kx, vx = split_kv(kv_ref[...], 0, bias_ref)
    tile(q_ref, kx, vx, put(acc_ref))


def attend_first(order, adjacency, mine, kv):
    return pl.pallas_call(
        first_kernel,
        out_shape=(WIDE, jax.ShapeDtypeStruct((NZ, NK // BLOCK, 128), F32), ACC),
        in_specs=[SMEM, VMEM, VMEM, VMEM],
        out_specs=(VMEM, VMEM, VMEM),
        scratch_shapes=[pltpu.VMEM((64, 128), F32), pltpu.VMEM((128, 128), F32)],
        compiler_params=PARAMS,
        cost_estimate=cost(NK),
        name="attend_first",
    )(order, adjacency, mine, kv)


def both_tiles(step, bias_ref, low_ref, high_ref, kx_ref, vx_ref, pairs):
    kx_ref[0], vx_ref[0] = split_kv(low_ref[...], -step, bias_ref)
    kx_ref[1], vx_ref[1] = split_kv(high_ref[...], step, bias_ref)

    def body(n, carry):
        kx, vx = kx_ref[n], vx_ref[n]
        for q_ref, acc_ref in pairs:
            tile(q_ref, kx, vx, add(acc_ref))
        return carry

    lax.fori_loop(0, 2, body, 0)


SPLIT = [pltpu.VMEM((2, NK, 128), BF16), pltpu.VMEM((2, NK, 128), BF16)]


def second_kernel(
    q_ref, other_ref, bias_ref, kv_ref, low_ref, high_ref, acc_in, q2_ref, acc_ref, acc2_ref, kx_ref, vx_ref
):
    widen(other_ref, 8, q2_ref)
    kx, vx = split_kv(kv_ref[...], 0, bias_ref)
    tile(q2_ref, kx, vx, put(acc2_ref))
    both_tiles(1, bias_ref, low_ref, high_ref, kx_ref, vx_ref, ((q_ref, acc_ref), (q2_ref, acc2_ref)))


def attend_second(q, other, bias, kv, low, high, acc):
    return pl.pallas_call(
        second_kernel,
        out_shape=(WIDE, ACC, ACC),
        in_specs=[VMEM] * 7,
        out_specs=(VMEM, VMEM, VMEM),
        scratch_shapes=SPLIT,
        input_output_aliases={6: 1},
        compiler_params=PARAMS,
        cost_estimate=cost(5 * NK),
        name="attend_second",
    )(q, other, bias, kv, low, high, acc)


def middle_kernel(step, q_ref, q2_ref, bias_ref, low_ref, high_ref, in1, in2, acc_ref, acc2_ref, kx_ref, vx_ref):
    both_tiles(step, bias_ref, low_ref, high_ref, kx_ref, vx_ref, ((q_ref, acc_ref), (q2_ref, acc2_ref)))


def attend_middle(step, q, q2, bias, low, high, acc, acc2):
    return pl.pallas_call(
        lambda *refs: middle_kernel(step, *refs),
        out_shape=(ACC, ACC),
        in_specs=[VMEM] * 7,
        out_specs=(VMEM, VMEM),
        scratch_shapes=SPLIT,
        input_output_aliases={5: 0, 6: 1},
        compiler_params=PARAMS,
        cost_estimate=cost(4 * NK),
        name="attend_middle",
    )(q, q2, bias, low, high, acc, acc2)


HALF = NQ // 2
SUMS = 16


def split_last(low_ref, high_ref, bias_ref):
    return split_kv(jnp.concatenate([low_ref[...], high_ref[...]], axis=0), NZ // 2, bias_ref)


def last_other_kernel(q_ref, bias_ref, low_ref, high_ref, in_ref, message_ref, acc_ref):
    def store(rows, part):
        acc_ref[rows, :] = in_ref[rows, :] + part

    tile(q_ref, *split_last(low_ref, high_ref, bias_ref), store)
    lane = lax.broadcasted_iota(jnp.int32, (BLOCK, 128), 1)
    row = lax.broadcasted_iota(jnp.int32, (SUMS, 128), 0)
    column = lax.broadcasted_iota(jnp.int32, (SUMS, 128), 1)
    sums = jnp.zeros((SUMS, BLOCK), F32)
    blocks = [acc_ref[n * BLOCK : (n + 1) * BLOCK, :] for n in range(8)]
    for m in range(NY):
        pair = jnp.where(lane < HD, pltpu.roll(blocks[2 * m], 64, 1), blocks[2 * m + 1])
        message_ref[m * BLOCK : (m + 1) * BLOCK, :] = pair.astype(BF16)
    for n in range(8):
        coarse = blocks[n].astype(BF16).astype(F32)
        spread = jnp.where(lane == 0, coarse, jnp.where(lane == 1, blocks[n] - coarse, 0.0)).astype(BF16)
        at = jnp.where((row // 2 == n) & (row % 2 == column), 1.0, 0.0).astype(BF16)
        sums += lax.dot_general(at, spread, (((1,), (1,)), ((), ())), preferred_element_type=F32)
    message_ref[HALF:, :] = sums.astype(BF16)


def attend_last_other(q2, bias, low, high, acc2):
    return pl.pallas_call(
        last_other_kernel,
        out_shape=jax.ShapeDtypeStruct((HALF + SUMS, 128), BF16),
        in_specs=[VMEM] * 5,
        out_specs=VMEM,
        scratch_shapes=[pltpu.VMEM((NQ, 128), F32)],
        compiler_params=PARAMS,
        cost_estimate=cost(NK),
        name="attend_last_other",
    )(q2, bias, low, high, acc2)


def last_mine_kernel(q_ref, bias_ref, low_ref, high_ref, in_ref, acc_ref):
    tile(q_ref, *split_last(low_ref, high_ref, bias_ref), add(acc_ref))


def attend_last_mine(q, bias, low, high, acc):
    return pl.pallas_call(
        last_mine_kernel,
        out_shape=ACC,
        in_specs=[VMEM] * 5,
        out_specs=VMEM,
        input_output_aliases={4: 0},
        compiler_params=PARAMS,
        cost_estimate=cost(NK),
        name="attend_last_mine",
    )(q, bias, low, high, acc)


def finish_kernel(mine_ref, message_ref, *out_refs):
    lane = lax.broadcasted_iota(jnp.int32, (BLOCK, 128), 1)
    row = lax.broadcasted_iota(jnp.int32, (SUMS, 128), 0)
    sums = message_ref[HALF:, :]
    blocks = [mine_ref[n * BLOCK : (n + 1) * BLOCK, :] for n in range(8)]
    spread = []
    for n in range(8):
        at = jnp.where(row // 2 == n, 1.0, 0.0).astype(BF16)
        spread.append(lax.dot_general(sums, at, (((0,), (0,)), ((), ())), preferred_element_type=F32))
    for m in range(NY):
        one, two = blocks[2 * m], blocks[2 * m + 1]
        total = jnp.where(lane < HD, pltpu.roll(one, 64, 1), two)
        total += message_ref[m * BLOCK : (m + 1) * BLOCK, :].astype(F32)
        weight = jnp.where(lane < HD, one + spread[2 * m], pltpu.roll(two, 64, 1) + spread[2 * m + 1])
        out_refs[m][...] = (total / weight).astype(BF16)


def finish(mine, message):
    return pl.pallas_call(
        finish_kernel,
        out_shape=[jax.ShapeDtypeStruct((BLOCK, 128), BF16)] * NY,
        in_specs=[VMEM, VMEM],
        out_specs=[VMEM] * NY,
        compiler_params=PARAMS,
        name="finish",
    )(mine, message)


def output_kernel(a_ref, own_ref, near_ref, far_ref, out_ref, w_ref):
    y, xl, core = (lax.axis_index(a).astype(jnp.int32) for a in ("y", "xl", "core"))
    for side, turn, piece in (
        (xl, core, own_ref[...]),
        (xl, 1 - core, near_ref[...]),
        (1 - xl, core, far_ref[:256, :]),
        (1 - xl, 1 - core, far_ref[256:, :]),
    ):
        w_ref[pl.ds(pl.multiple_of((2 * side + turn) * 256, 256), 256), :] = piece
    lane = lax.broadcasted_iota(jnp.int32, (BLOCK, 128), 1)
    lefts, rights, weights = [], [], []
    for source in range(4):
        for s in range(4):
            pair = a_ref[4 * source + s].astype(F32)
            lefts.append(jnp.where(lane < HD, pair, 0.0).astype(BF16))
            rights.append(jnp.where(lane < HD, 0.0, pair).astype(BF16))
            j = lax.rem(y + s, NY)
            row = pl.multiple_of(source * 256 + j * HD, HD)
            w = w_ref[pl.ds(row, HD), :]
            weights += [w, w]
    w = jnp.concatenate(weights, axis=0)
    out_ref[:BLOCK, :] = jnp.dot(jnp.concatenate(lefts, axis=1), w, preferred_element_type=F32).astype(BF16)
    out_ref[BLOCK:, :] = jnp.dot(jnp.concatenate(rights, axis=1), w, preferred_element_type=F32).astype(BF16)


def output(attended, own, near, far):
    return pl.pallas_call(
        output_kernel,
        out_shape=jax.ShapeDtypeStruct((ROWS, 256), BF16),
        in_specs=[VMEM] * 4,
        out_specs=VMEM,
        scratch_shapes=[pltpu.VMEM((1024, 256), BF16)],
        compiler_params=PARAMS,
        name="output",
    )(attended, own, near, far)


def shards(tokens, gain, w_query, w_key, w_value, w_out, temper, adjacency, order):
    whole = lax.all_gather(tokens, HEAD, axis=1, tiled=True)
    messages = project(whole, gain[None, :], w_query, w_key, w_value, temper)
    got = jnp.stack([messages[0]] + [lax.ppermute(messages[s], "y", ring(NY, s)) for s in range(1, NY)])
    kv = got[:, :ROWS, :].reshape(NK, 128)
    query = got[:, ROWS:, :]
    query, kv = lax.optimization_barrier((query, kv))
    low, high = lax.ppermute(kv, "z", ring(NZ, 1)), lax.ppermute(kv, "z", ring(NZ, -1))
    other = lax.ppermute(query, "xh", [(0, 1), (1, 0)])
    q, bias, acc = attend_first(order, adjacency, query, kv)
    xl, core = lax.axis_index("xl"), lax.axis_index("core")
    block = lambda side, turn: lax.dynamic_slice_in_dim(w_out, (2 * side + turn) * 256, 256, 1)
    own, relayed = block(xl, core), block(1 - xl, core)
    near = jnp.concatenate([block(xl, 1 - core), block(1 - xl, 1 - core)], axis=0)
    for step in (1, 2, 3):
        low, high, acc, near = lax.optimization_barrier((low, high, acc, near))
        if step < 3:
            next_low, next_high = lax.ppermute(low, "z", ring(NZ, 1)), lax.ppermute(high, "z", ring(NZ, -1))
        else:
            next_low = lax.ppermute(low[: NK // 2], "z", ring(NZ, 1))
            next_high = lax.ppermute(high[NK // 2 :], "z", ring(NZ, -1))
        if step == 1:
            q2, acc, acc2 = attend_second(q, other, bias, kv, low, high, acc)
        else:
            acc, acc2 = attend_middle(step, q, q2, bias, low, high, acc, acc2)
        low, high = next_low, next_high
        if step == 1:
            near = lax.ppermute(near, "core", ring(NCORE, 1))
        if step == 2:
            far = lax.ppermute(jnp.concatenate([relayed, near[256:]], axis=0), "xl", ring(NXL, 1))
            near = near[:256]
    low, high, acc, own, near, far = lax.optimization_barrier((low, high, acc, own, near, far))
    message = attend_last_other(q2, bias, low, high, acc2)
    message, acc = lax.optimization_barrier((message, acc))
    message = lax.ppermute(message, "xh", [(0, 1), (1, 0)])
    attended = finish(attend_last_mine(q, bias, low, high, acc), message)
    back = jnp.stack([attended[0]] + [lax.ppermute(attended[s], "y", ring(NY, -s)) for s in range(1, NY)])
    gathered = lax.all_gather(back, HEAD, axis=0, tiled=True)
    return output(gathered, own, near, far)


def solution(mesh):
    fine = Mesh(mesh.devices.reshape(NXH, NZ, NY, NXL, NCORE), CTX + HEAD)
    in_specs = (
        P(CTX, HEAD),
        P(),
        P(None, HEAD),
        P(None, HEAD),
        P(None, HEAD),
        P(HEAD, None),
        P(HEAD),
        P(),
        P(),
    )
    return jax.shard_map(shards, mesh=fine, in_specs=in_specs, out_specs=P(CTX, HEAD), check_vma=False)
```

```python
import jax
import jax.numpy as jnp
from jax import lax
from jax.experimental import pallas as pl
from jax.experimental.pallas import tpu as pltpu
from jax.sharding import Mesh, PartitionSpec as P

CTX = ("xh", "z", "y")
HEAD = ("xl", "core")
NXH, NZ, NY, NXL, NCORE = 2, 8, 4, 2, 2
BLOCK = 128
HD = 64
ROWS = 256
EPS = 1e-06
LOG2E = 1.4426950408889634
DEAD = -30000.0
F32 = jnp.float32
BF16 = jnp.bfloat16
VMEM = pl.BlockSpec(memory_space=pltpu.VMEM)
SMEM = pl.BlockSpec(memory_space=pltpu.SMEM)
HBM = pl.BlockSpec(memory_space=pltpu.HBM)
PARAMS = pltpu.CompilerParams(vmem_limit_bytes=32 << 20)


def ring(length, by):
    return [(i, (i + by) % length) for i in range(length)]


def project_kernel(
    x_ref, temper_hbm, gain_hbm, wq_hbm, wk_hbm, wv_hbm, *refs
):
    out_refs, (stage_ref, temper_ref, gain_ref, wq_ref, wk_ref, wv_ref, sems) = refs[:NY], refs[NY:]
    pairs = (
        (gain_hbm, gain_ref),
        (wq_hbm, wq_ref),
        (wk_hbm, wk_ref),
        (wv_hbm, wv_ref),
        (temper_hbm, temper_ref),
    )
    copies = [pltpu.make_async_copy(source, target, sems.at[n]) for n, (source, target) in enumerate(pairs)]
    for copy in copies:
        copy.start()
    x = x_ref[...].astype(F32)
    scaled = x * lax.rsqrt(jnp.mean(x * x, axis=-1, keepdims=True) + EPS)
    copies[0].wait()
    normed = (scaled * gain_ref[...]).astype(BF16)
    copies[1].wait()
    query = jnp.dot(normed, wq_ref[...], preferred_element_type=F32)
    copies[2].wait()
    keys = jnp.dot(normed, wk_ref[...], preferred_element_type=F32)
    copies[3].wait()
    values = jnp.dot(normed, wv_ref[...], preferred_element_type=F32)

    copies[4].wait()

    def unit(part):
        return part * lax.rsqrt(jnp.mean(part * part, axis=-1, keepdims=True) + EPS)

    for j in range(4):
        cols = slice(HD * j, HD * (j + 1))
        q = unit(query[:, cols]) * (temper_ref[j] * (LOG2E / HD))
        k = unit(keys[:, cols])
        v = values[:, cols]
        stage_ref[j, :ROWS, :] = jnp.concatenate([k, v], axis=1).astype(BF16)
        stage_ref[j, ROWS:, :] = jnp.concatenate([q[:BLOCK], q[BLOCK:]], axis=1).astype(BF16)
    y = lax.axis_index("y").astype(jnp.int32)
    for s in range(NY):
        out_refs[s][...] = stage_ref[lax.rem(y + s, NY)]


def project(whole, gain, w_query, w_key, w_value, temper):
    hold = lambda x: pltpu.with_memory_space_constraint(x, pltpu.HBM)
    return pl.pallas_call(
        project_kernel,
        out_shape=[jax.ShapeDtypeStruct((ROWS + BLOCK, 128), BF16)] * NY,
        in_specs=[VMEM, HBM, HBM, HBM, HBM, HBM],
        out_specs=[VMEM] * NY,
        scratch_shapes=[
            pltpu.VMEM((NY, ROWS + BLOCK, 128), BF16),
            pltpu.SMEM((4,), F32),
            pltpu.VMEM((1, 1024), F32),
            pltpu.VMEM((1024, 256), BF16),
            pltpu.VMEM((1024, 256), BF16),
            pltpu.VMEM((1024, 256), BF16),
            pltpu.SemaphoreType.DMA((5,)),
        ],
        compiler_params=PARAMS,
        name="project",
    )(whole, hold(temper), hold(gain), hold(w_query), hold(w_key), hold(w_value))


QT = 256
NQ = 1024
NK = 1024


def widen(packed_ref, first, out_ref):
    lane = lax.broadcasted_iota(jnp.int32, (BLOCK, 128), 1)
    for m in range(NY):
        pair = packed_ref[m].astype(F32)
        for b in range(2):
            part = pair if b == 0 else pltpu.roll(pair, 64, 1)
            flag = jnp.where(lane == HD + first + 2 * m + b, 1.0, 0.0)
            at = (2 * m + b) * BLOCK
            out_ref[at : at + BLOCK, :] = jnp.where(lane < HD, part, flag).astype(BF16)


def bias_rows(order_ref, adjacency_ref, keys_ref, queries_ref, bias_ref):
    z, y, xh = (lax.axis_index(a).astype(jnp.int32) for a in ("z", "y", "xh"))
    lane = lax.broadcasted_iota(jnp.int32, (1, 128), 1)

    def pick(side, zs, s, b):
        block = 2 * ((side * NZ + zs) * NY + lax.rem(y - s + NY, NY)) + b
        return jnp.where(lane == order_ref[block], 1.0, 0.0)

    queries_ref[...] = jnp.zeros_like(queries_ref)
    for s in range(NY):
        for b in range(2):
            n = 2 * s + b
            queries_ref[HD + n : HD + n + 1, :] = pick(xh, z, s, b)
            queries_ref[HD + 8 + n : HD + 9 + n, :] = pick(1 - xh, z, s, b)
            for zs in range(NZ):
                keys_ref[8 * zs + n : 8 * zs + n + 1, :] = pick(xh, zs, s, b)
    turned = (((1,), (1,)), ((), ()))
    adjacency = adjacency_ref[...].astype(F32).astype(BF16)
    keys, queries = keys_ref[...].astype(BF16), queries_ref[...].astype(BF16)
    picked = lax.dot_general(keys, adjacency, turned, preferred_element_type=F32).astype(BF16)
    live = lax.dot_general(picked, queries, turned, preferred_element_type=F32)
    bias_ref[...] = jnp.where(live > 0.5, 0.0, DEAD).reshape(NZ, NK // BLOCK, 128)


def chunk_at(distance):
    return lax.rem(lax.axis_index("z").astype(jnp.int32) + (distance + NZ), NZ)


def split_kv(kv, distance, bias_ref):
    lane = lax.broadcasted_iota(jnp.int32, (NK, 128), 1)
    kv = kv.astype(F32)
    table = bias_ref[chunk_at(distance)]
    bias = jnp.concatenate(
        [jnp.broadcast_to(table[b : b + 1, :], (BLOCK, 128)) for b in range(NK // BLOCK)], axis=0
    )
    return jnp.where(lane < HD, kv, bias).astype(BF16), jnp.where(lane < HD, 1.0, kv).astype(BF16)


def tile(q_ref, kx, vx, store):
    for t in range(NQ // QT):
        rows = slice(t * QT, (t + 1) * QT)
        scores = lax.dot_general(q_ref[rows, :], kx, (((1,), (1,)), ((), ())), preferred_element_type=F32)
        probs = jnp.exp2(scores).astype(BF16)
        store(rows, jnp.dot(probs, vx, preferred_element_type=F32))


def put(ref):
    def store(rows, part):
        ref[rows, :] = part

    return store


def add(ref):
    def store(rows, part):
        ref[rows, :] += part

    return store


def cost(keys):
    return pl.CostEstimate(flops=512 * NQ * keys, transcendentals=NQ * keys, bytes_accessed=4 << 20)


ACC = jax.ShapeDtypeStruct((NQ, 128), F32)
WIDE = jax.ShapeDtypeStruct((NQ, 128), BF16)


def first_kernel(order_ref, adjacency_ref, mine_ref, kv_ref, q_ref, bias_ref, acc_ref, keys_ref, queries_ref):
    bias_rows(order_ref, adjacency_ref, keys_ref, queries_ref, bias_ref)
    widen(mine_ref, 0, q_ref)
    kx, vx = split_kv(kv_ref[...], 0, bias_ref)
    tile(q_ref, kx, vx, put(acc_ref))


def attend_first(order, adjacency, mine, kv):
    return pl.pallas_call(
        first_kernel,
        out_shape=(WIDE, jax.ShapeDtypeStruct((NZ, NK // BLOCK, 128), F32), ACC),
        in_specs=[SMEM, VMEM, VMEM, VMEM],
        out_specs=(VMEM, VMEM, VMEM),
        scratch_shapes=[pltpu.VMEM((64, 128), F32), pltpu.VMEM((128, 128), F32)],
        compiler_params=PARAMS,
        cost_estimate=cost(NK),
        name="attend_first",
    )(order, adjacency, mine, kv)


def both_tiles(step, bias_ref, low_ref, high_ref, kx_ref, vx_ref, pairs):
    kx_ref[:NK, :], vx_ref[:NK, :] = split_kv(low_ref[...], -step, bias_ref)
    kx_ref[NK:, :], vx_ref[NK:, :] = split_kv(high_ref[...], step, bias_ref)
    for q_ref, acc_ref in pairs:
        tile(q_ref, kx_ref[...], vx_ref[...], add(acc_ref))


SPLIT = [pltpu.VMEM((2 * NK, 128), BF16), pltpu.VMEM((2 * NK, 128), BF16)]


def second_kernel(q_ref, other_ref, bias_ref, low_ref, high_ref, acc_in, q2_ref, acc_ref, acc2_ref, kx_ref, vx_ref):
    widen(other_ref, 8, q2_ref)
    acc2_ref[...] = jnp.zeros_like(acc2_ref)
    both_tiles(1, bias_ref, low_ref, high_ref, kx_ref, vx_ref, ((q_ref, acc_ref), (q2_ref, acc2_ref)))


def attend_second(q, other, bias, low, high, acc):
    return pl.pallas_call(
        second_kernel,
        out_shape=(WIDE, ACC, ACC),
        in_specs=[VMEM] * 6,
        out_specs=(VMEM, VMEM, VMEM),
        scratch_shapes=SPLIT,
        input_output_aliases={5: 1},
        compiler_params=PARAMS,
        cost_estimate=cost(4 * NK),
        name="attend_second",
    )(q, other, bias, low, high, acc)


def third_kernel(q_ref, q2_ref, bias_ref, kv_ref, low_ref, high_ref, in1, in2, acc_ref, acc2_ref, kx_ref, vx_ref):
    both_tiles(2, bias_ref, low_ref, high_ref, kx_ref, vx_ref, ((q_ref, acc_ref), (q2_ref, acc2_ref)))
    tile(q2_ref, *split_kv(kv_ref[...], 0, bias_ref), add(acc2_ref))


def attend_third(q, q2, bias, kv, low, high, acc, acc2):
    return pl.pallas_call(
        third_kernel,
        out_shape=(ACC, ACC),
        in_specs=[VMEM] * 8,
        out_specs=(VMEM, VMEM),
        scratch_shapes=SPLIT,
        input_output_aliases={6: 0, 7: 1},
        compiler_params=PARAMS,
        cost_estimate=cost(5 * NK),
        name="attend_third",
    )(q, q2, bias, kv, low, high, acc, acc2)


def fourth_other_kernel(q_ref, bias_ref, low_ref, high_ref, acc_in, acc_ref, kx_ref, vx_ref):
    both_tiles(3, bias_ref, low_ref, high_ref, kx_ref, vx_ref, ((q_ref, acc_ref),))


def attend_fourth_other(q2, bias, low, high, acc2):
    return pl.pallas_call(
        fourth_other_kernel,
        out_shape=ACC,
        in_specs=[VMEM] * 5,
        out_specs=VMEM,
        scratch_shapes=SPLIT,
        input_output_aliases={4: 0},
        compiler_params=PARAMS,
        cost_estimate=cost(2 * NK),
        name="attend_fourth_other",
    )(q2, bias, low, high, acc2)


HALF = NQ // 2
SUMS = 16


def split_last(low_ref, high_ref, bias_ref):
    return split_kv(jnp.concatenate([low_ref[...], high_ref[...]], axis=0), NZ // 2, bias_ref)


def last_other_kernel(q_ref, bias_ref, low_ref, high_ref, in_ref, message_ref, acc_ref):
    def store(rows, part):
        acc_ref[rows, :] = in_ref[rows, :] + part

    tile(q_ref, *split_last(low_ref, high_ref, bias_ref), store)
    lane = lax.broadcasted_iota(jnp.int32, (BLOCK, 128), 1)
    row = lax.broadcasted_iota(jnp.int32, (SUMS, 128), 0)
    column = lax.broadcasted_iota(jnp.int32, (SUMS, 128), 1)
    sums = jnp.zeros((SUMS, BLOCK), F32)
    blocks = [acc_ref[n * BLOCK : (n + 1) * BLOCK, :] for n in range(8)]
    for m in range(NY):
        pair = jnp.where(lane < HD, pltpu.roll(blocks[2 * m], 64, 1), blocks[2 * m + 1])
        message_ref[m * BLOCK : (m + 1) * BLOCK, :] = pair.astype(BF16)
    for n in range(8):
        coarse = blocks[n].astype(BF16).astype(F32)
        spread = jnp.where(lane == 0, coarse, jnp.where(lane == 1, blocks[n] - coarse, 0.0)).astype(BF16)
        at = jnp.where((row // 2 == n) & (row % 2 == column), 1.0, 0.0).astype(BF16)
        sums += lax.dot_general(at, spread, (((1,), (1,)), ((), ())), preferred_element_type=F32)
    message_ref[HALF:, :] = sums.astype(BF16)


def attend_last_other(q2, bias, low, high, acc2):
    return pl.pallas_call(
        last_other_kernel,
        out_shape=jax.ShapeDtypeStruct((HALF + SUMS, 128), BF16),
        in_specs=[VMEM] * 5,
        out_specs=VMEM,
        scratch_shapes=[pltpu.VMEM((NQ, 128), F32)],
        compiler_params=PARAMS,
        cost_estimate=cost(NK),
        name="attend_last_other",
    )(q2, bias, low, high, acc2)


def last_mine_kernel(q_ref, bias_ref, low_ref, high_ref, far_low, far_high, acc_in, acc_ref, kx_ref, vx_ref):
    both_tiles(3, bias_ref, low_ref, high_ref, kx_ref, vx_ref, ((q_ref, acc_ref),))
    tile(q_ref, *split_last(far_low, far_high, bias_ref), add(acc_ref))


def attend_last_mine(q, bias, low, high, far_low, far_high, acc):
    return pl.pallas_call(
        last_mine_kernel,
        out_shape=ACC,
        in_specs=[VMEM] * 7,
        out_specs=VMEM,
        scratch_shapes=SPLIT,
        input_output_aliases={6: 0},
        compiler_params=PARAMS,
        cost_estimate=cost(3 * NK),
        name="attend_last_mine",
    )(q, bias, low, high, far_low, far_high, acc)


def finish_kernel(mine_ref, message_ref, *out_refs):
    lane = lax.broadcasted_iota(jnp.int32, (BLOCK, 128), 1)
    row = lax.broadcasted_iota(jnp.int32, (SUMS, 128), 0)
    sums = message_ref[HALF:, :]
    blocks = [mine_ref[n * BLOCK : (n + 1) * BLOCK, :] for n in range(8)]
    spread = []
    for n in range(8):
        at = jnp.where(row // 2 == n, 1.0, 0.0).astype(BF16)
        spread.append(lax.dot_general(sums, at, (((0,), (0,)), ((), ())), preferred_element_type=F32))
    for m in range(NY):
        one, two = blocks[2 * m], blocks[2 * m + 1]
        total = jnp.where(lane < HD, pltpu.roll(one, 64, 1), two)
        total += message_ref[m * BLOCK : (m + 1) * BLOCK, :].astype(F32)
        weight = jnp.where(lane < HD, one + spread[2 * m], pltpu.roll(two, 64, 1) + spread[2 * m + 1])
        out_refs[m][...] = (total / weight).astype(BF16)


def finish(mine, message):
    return pl.pallas_call(
        finish_kernel,
        out_shape=[jax.ShapeDtypeStruct((BLOCK, 128), BF16)] * NY,
        in_specs=[VMEM, VMEM],
        out_specs=[VMEM] * NY,
        compiler_params=PARAMS,
        name="finish",
    )(mine, message)


def output_kernel(a_ref, own_ref, near_ref, far_ref, out_ref, w_ref):
    y, xl, core = (lax.axis_index(a).astype(jnp.int32) for a in ("y", "xl", "core"))
    for side, turn, piece in (
        (xl, core, own_ref[...]),
        (xl, 1 - core, near_ref[...]),
        (1 - xl, core, far_ref[:256, :]),
        (1 - xl, 1 - core, far_ref[256:, :]),
    ):
        w_ref[pl.ds(pl.multiple_of((2 * side + turn) * 256, 256), 256), :] = piece
    lane = lax.broadcasted_iota(jnp.int32, (BLOCK, 128), 1)
    lefts, rights, weights = [], [], []
    for source in range(4):
        for s in range(4):
            pair = a_ref[4 * source + s].astype(F32)
            lefts.append(jnp.where(lane < HD, pair, 0.0).astype(BF16))
            rights.append(jnp.where(lane < HD, 0.0, pair).astype(BF16))
            j = lax.rem(y + s, NY)
            row = pl.multiple_of(source * 256 + j * HD, HD)
            w = w_ref[pl.ds(row, HD), :]
            weights += [w, w]
    w = jnp.concatenate(weights, axis=0)
    out_ref[:BLOCK, :] = jnp.dot(jnp.concatenate(lefts, axis=1), w, preferred_element_type=F32).astype(BF16)
    out_ref[BLOCK:, :] = jnp.dot(jnp.concatenate(rights, axis=1), w, preferred_element_type=F32).astype(BF16)


def output(attended, own, near, far):
    return pl.pallas_call(
        output_kernel,
        out_shape=jax.ShapeDtypeStruct((ROWS, 256), BF16),
        in_specs=[VMEM] * 4,
        out_specs=VMEM,
        scratch_shapes=[pltpu.VMEM((1024, 256), BF16)],
        compiler_params=PARAMS,
        name="output",
    )(attended, own, near, far)


def shards(tokens, gain, w_query, w_key, w_value, w_out, temper, adjacency, order):
    whole = lax.all_gather(tokens, HEAD, axis=1, tiled=True)
    messages = project(whole, gain[None, :], w_query, w_key, w_value, temper)
    xl, core = lax.axis_index("xl"), lax.axis_index("core")
    w_out, messages = lax.optimization_barrier((w_out, messages))
    block = lambda side, turn: lax.dynamic_slice_in_dim(w_out, (2 * side + turn) * 256, 256, 1)
    own, relayed = block(xl, core), block(1 - xl, core)
    near = jnp.concatenate([block(xl, 1 - core), block(1 - xl, 1 - core)], axis=0)
    near = lax.ppermute(near, "core", ring(NCORE, 1))
    turned = {s: lax.ppermute(messages[s], "y", ring(NY, s)) for s in (2, 1, 3)}
    got = jnp.stack([messages[0]] + [turned[s] for s in range(1, NY)])
    kv = got[:, :ROWS, :].reshape(NK, 128)
    query = got[:, ROWS:, :]
    query, kv, near = lax.optimization_barrier((query, kv, near))
    up = lambda part: lax.ppermute(part, "z", ring(NZ, 1))
    down = lambda part: lax.ppermute(part, "z", ring(NZ, -1))
    low, high = up(kv), down(kv)
    other = lax.ppermute(query, "xh", ring(NXH, 1))
    q, bias, acc = attend_first(order, adjacency, query, kv)
    low, high, acc = lax.optimization_barrier((low, high, acc))
    low2, high2 = up(low), down(high)
    q2, acc, acc2 = attend_second(q, other, bias, low, high, acc)
    low2, high2, acc, near = lax.optimization_barrier((low2, high2, acc, near))
    low3, high3 = up(low2), down(high2)
    far = lax.ppermute(jnp.concatenate([relayed, near[256:]], axis=0), "xl", ring(NXL, 1))
    acc, acc2 = attend_third(q, q2, bias, kv, low2, high2, acc, acc2)
    low3, high3, acc2 = lax.optimization_barrier((low3, high3, acc2))
    low4, high4 = up(low3[: NK // 2]), down(high3[NK // 2 :])
    acc2 = attend_fourth_other(q2, bias, low3, high3, acc2)
    low4, high4, acc2, far = lax.optimization_barrier((low4, high4, acc2, far))
    message = attend_last_other(q2, bias, low4, high4, acc2)
    message, acc = lax.optimization_barrier((message, acc))
    message = lax.ppermute(message, "xh", ring(NXH, 1))
    attended = finish(attend_last_mine(q, bias, low3, high3, low4, high4, acc), message)
    back = jnp.stack([attended[0]] + [lax.ppermute(attended[s], "y", ring(NY, -s)) for s in range(1, NY)])
    gathered = lax.all_gather(back, HEAD, axis=0, tiled=True)
    return output(gathered, own, near[:256], far)


def solution(mesh):
    fine = Mesh(mesh.devices.reshape(NXH, NZ, NY, NXL, NCORE), CTX + HEAD)
    in_specs = (
        P(CTX, HEAD),
        P(),
        P(None, HEAD),
        P(None, HEAD),
        P(None, HEAD),
        P(HEAD, None),
        P(HEAD),
        P(),
        P(),
    )
    return jax.shard_map(shards, mesh=fine, in_specs=in_specs, out_specs=P(CTX, HEAD), check_vma=False)
```

```python
import jax
import jax.numpy as jnp
from jax import lax
from jax.experimental import pallas as pl
from jax.experimental.pallas import tpu as pltpu
from jax.sharding import Mesh, PartitionSpec as P

CTX = ("xh", "z", "y")
HEAD = ("xl", "core")
NXH, NZ, NY, NXL, NCORE = 2, 8, 4, 2, 2
BLOCK = 128
HD = 64
ROWS = 256
EPS = 1e-06
LOG2E = 1.4426950408889634
DEAD = -30000.0
F32 = jnp.float32
BF16 = jnp.bfloat16
VMEM = pl.BlockSpec(memory_space=pltpu.VMEM)
SMEM = pl.BlockSpec(memory_space=pltpu.SMEM)
HBM = pl.BlockSpec(memory_space=pltpu.HBM)
PARAMS = pltpu.CompilerParams(vmem_limit_bytes=32 << 20)


def ring(length, by):
    return [(i, (i + by) % length) for i in range(length)]


def project_kernel(
    x_ref, temper_hbm, gain_hbm, wq_hbm, wk_hbm, wv_hbm, *refs
):
    out_refs, (stage_ref, temper_ref, gain_ref, wq_ref, wk_ref, wv_ref, sems) = refs[:NY], refs[NY:]
    pairs = (
        (gain_hbm, gain_ref),
        (wq_hbm, wq_ref),
        (wk_hbm, wk_ref),
        (wv_hbm, wv_ref),
        (temper_hbm, temper_ref),
    )
    copies = [pltpu.make_async_copy(source, target, sems.at[n]) for n, (source, target) in enumerate(pairs)]
    for copy in copies:
        copy.start()
    x = x_ref[...].astype(F32)
    scaled = x * lax.rsqrt(jnp.mean(x * x, axis=-1, keepdims=True) + EPS)
    copies[0].wait()
    normed = (scaled * gain_ref[...]).astype(BF16)
    copies[1].wait()
    query = jnp.dot(normed, wq_ref[...], preferred_element_type=F32)
    copies[2].wait()
    keys = jnp.dot(normed, wk_ref[...], preferred_element_type=F32)
    copies[3].wait()
    values = jnp.dot(normed, wv_ref[...], preferred_element_type=F32)

    copies[4].wait()

    lower = lax.broadcasted_iota(jnp.int32, (ROWS, 128), 1) < HD
    head = lower[:BLOCK]

    def unit(pair, first=1.0, second=1.0):
        square = pair * pair
        low = jnp.sum(jnp.where(lower, square, 0.0), axis=-1, keepdims=True)
        high = jnp.sum(jnp.where(lower, 0.0, square), axis=-1, keepdims=True)
        low = lax.rsqrt(low / HD + EPS) * first
        high = lax.rsqrt(high / HD + EPS) * second
        return pair * jnp.where(lower, low, high)

    for n in range(2):
        j = 2 * n
        cols = slice(128 * n, 128 * (n + 1))
        q = unit(query[:, cols], temper_ref[j] * (LOG2E / HD), temper_ref[j + 1] * (LOG2E / HD))
        k = unit(keys[:, cols])
        v = values[:, cols]
        stage_ref[j, :ROWS, :] = jnp.where(lower, k, pltpu.roll(v, 64, 1)).astype(BF16)
        stage_ref[j + 1, :ROWS, :] = jnp.where(lower, pltpu.roll(k, 64, 1), v).astype(BF16)
        one, two = q[:BLOCK], q[BLOCK:]
        stage_ref[j, ROWS:, :] = jnp.where(head, one, pltpu.roll(two, 64, 1)).astype(BF16)
        stage_ref[j + 1, ROWS:, :] = jnp.where(head, pltpu.roll(one, 64, 1), two).astype(BF16)
    y = lax.axis_index("y").astype(jnp.int32)
    for s in range(NY):
        out_refs[s][...] = stage_ref[lax.rem(y + s, NY)]


def project(whole, gain, w_query, w_key, w_value, temper):
    hold = lambda x: pltpu.with_memory_space_constraint(x, pltpu.HBM)
    return pl.pallas_call(
        project_kernel,
        out_shape=[jax.ShapeDtypeStruct((ROWS + BLOCK, 128), BF16)] * NY,
        in_specs=[VMEM, HBM, HBM, HBM, HBM, HBM],
        out_specs=[VMEM] * NY,
        scratch_shapes=[
            pltpu.VMEM((NY, ROWS + BLOCK, 128), BF16),
            pltpu.SMEM((4,), F32),
            pltpu.VMEM((1, 1024), F32),
            pltpu.VMEM((1024, 256), BF16),
            pltpu.VMEM((1024, 256), BF16),
            pltpu.VMEM((1024, 256), BF16),
            pltpu.SemaphoreType.DMA((5,)),
        ],
        compiler_params=PARAMS,
        name="project",
    )(whole, hold(temper), hold(gain), hold(w_query), hold(w_key), hold(w_value))


QT = 256
NQ = 1024
NK = 1024


def widen(packed_ref, first, out_ref):
    lane = lax.broadcasted_iota(jnp.int32, (BLOCK, 128), 1)
    for m in range(NY):
        pair = packed_ref[m].astype(F32)
        for b in range(2):
            part = pair if b == 0 else pltpu.roll(pair, 64, 1)
            flag = jnp.where(lane == HD + first + 2 * m + b, 1.0, 0.0)
            at = (2 * m + b) * BLOCK
            out_ref[at : at + BLOCK, :] = jnp.where(lane < HD, part, flag).astype(BF16)


def bias_rows(order_ref, adjacency_ref, keys_ref, queries_ref, bias_ref):
    z, y, xh = (lax.axis_index(a).astype(jnp.int32) for a in ("z", "y", "xh"))
    lane = lax.broadcasted_iota(jnp.int32, (1, 128), 1)

    def pick(side, zs, s, b):
        block = 2 * ((side * NZ + zs) * NY + lax.rem(y - s + NY, NY)) + b
        return jnp.where(lane == order_ref[block], 1.0, 0.0)

    queries_ref[...] = jnp.zeros_like(queries_ref)
    for s in range(NY):
        for b in range(2):
            n = 2 * s + b
            queries_ref[HD + n : HD + n + 1, :] = pick(xh, z, s, b)
            queries_ref[HD + 8 + n : HD + 9 + n, :] = pick(1 - xh, z, s, b)
            for zs in range(NZ):
                keys_ref[8 * zs + n : 8 * zs + n + 1, :] = pick(xh, zs, s, b)
    turned = (((1,), (1,)), ((), ()))
    adjacency = adjacency_ref[...].astype(F32).astype(BF16)
    keys, queries = keys_ref[...].astype(BF16), queries_ref[...].astype(BF16)
    picked = lax.dot_general(keys, adjacency, turned, preferred_element_type=F32).astype(BF16)
    live = lax.dot_general(picked, queries, turned, preferred_element_type=F32)
    bias_ref[...] = jnp.where(live > 0.5, 0.0, DEAD).reshape(NZ, NK // BLOCK, 128)


def chunk_at(distance):
    return lax.rem(lax.axis_index("z").astype(jnp.int32) + (distance + NZ), NZ)


def split_kv(kv, distance, bias_ref):
    lane = lax.broadcasted_iota(jnp.int32, (NK, 128), 1)
    kv = kv.astype(F32)
    table = bias_ref[chunk_at(distance)]
    bias = jnp.concatenate(
        [jnp.broadcast_to(table[b : b + 1, :], (BLOCK, 128)) for b in range(NK // BLOCK)], axis=0
    )
    return jnp.where(lane < HD, kv, bias).astype(BF16), jnp.where(lane < HD, 1.0, kv).astype(BF16)


def tile(q_ref, kx, vx, store):
    for t in range(NQ // QT):
        rows = slice(t * QT, (t + 1) * QT)
        scores = lax.dot_general(q_ref[rows, :], kx, (((1,), (1,)), ((), ())), preferred_element_type=F32)
        probs = jnp.exp2(scores).astype(BF16)
        store(rows, jnp.dot(probs, vx, preferred_element_type=F32))


def put(ref):
    def store(rows, part):
        ref[rows, :] = part

    return store


def add(ref):
    def store(rows, part):
        ref[rows, :] += part

    return store


def cost(keys):
    return pl.CostEstimate(flops=512 * NQ * keys, transcendentals=NQ * keys, bytes_accessed=4 << 20)


ACC = jax.ShapeDtypeStruct((NQ, 128), F32)
WIDE = jax.ShapeDtypeStruct((NQ, 128), BF16)


def first_kernel(order_ref, adjacency_ref, mine_ref, kv_ref, q_ref, bias_ref, acc_ref, keys_ref, queries_ref):
    bias_rows(order_ref, adjacency_ref, keys_ref, queries_ref, bias_ref)
    widen(mine_ref, 0, q_ref)
    kx, vx = split_kv(kv_ref[...], 0, bias_ref)
    tile(q_ref, kx, vx, put(acc_ref))


def attend_first(order, adjacency, mine, kv):
    return pl.pallas_call(
        first_kernel,
        out_shape=(WIDE, jax.ShapeDtypeStruct((NZ, NK // BLOCK, 128), F32), ACC),
        in_specs=[SMEM, VMEM, VMEM, VMEM],
        out_specs=(VMEM, VMEM, VMEM),
        scratch_shapes=[pltpu.VMEM((64, 128), F32), pltpu.VMEM((128, 128), F32)],
        compiler_params=PARAMS,
        cost_estimate=cost(NK),
        name="attend_first",
    )(order, adjacency, mine, kv)


def both_tiles(step, bias_ref, low_ref, high_ref, kx_ref, vx_ref, pairs):
    kx_ref[:NK, :], vx_ref[:NK, :] = split_kv(low_ref[...], -step, bias_ref)
    kx_ref[NK:, :], vx_ref[NK:, :] = split_kv(high_ref[...], step, bias_ref)
    for q_ref, acc_ref in pairs:
        tile(q_ref, kx_ref[...], vx_ref[...], add(acc_ref))


SPLIT = [pltpu.VMEM((2 * NK, 128), BF16), pltpu.VMEM((2 * NK, 128), BF16)]


def second_kernel(q_ref, other_ref, bias_ref, low_ref, high_ref, acc_in, q2_ref, acc_ref, acc2_ref, kx_ref, vx_ref):
    widen(other_ref, 8, q2_ref)
    acc2_ref[...] = jnp.zeros_like(acc2_ref)
    both_tiles(1, bias_ref, low_ref, high_ref, kx_ref, vx_ref, ((q_ref, acc_ref), (q2_ref, acc2_ref)))


def attend_second(q, other, bias, low, high, acc):
    return pl.pallas_call(
        second_kernel,
        out_shape=(WIDE, ACC, ACC),
        in_specs=[VMEM] * 6,
        out_specs=(VMEM, VMEM, VMEM),
        scratch_shapes=SPLIT,
        input_output_aliases={5: 1},
        compiler_params=PARAMS,
        cost_estimate=cost(4 * NK),
        name="attend_second",
    )(q, other, bias, low, high, acc)


def third_kernel(q_ref, q2_ref, bias_ref, kv_ref, low_ref, high_ref, in1, in2, acc_ref, acc2_ref, kx_ref, vx_ref):
    both_tiles(2, bias_ref, low_ref, high_ref, kx_ref, vx_ref, ((q_ref, acc_ref), (q2_ref, acc2_ref)))
    tile(q2_ref, *split_kv(kv_ref[...], 0, bias_ref), add(acc2_ref))


def attend_third(q, q2, bias, kv, low, high, acc, acc2):
    return pl.pallas_call(
        third_kernel,
        out_shape=(ACC, ACC),
        in_specs=[VMEM] * 8,
        out_specs=(VMEM, VMEM),
        scratch_shapes=SPLIT,
        input_output_aliases={6: 0, 7: 1},
        compiler_params=PARAMS,
        cost_estimate=cost(5 * NK),
        name="attend_third",
    )(q, q2, bias, kv, low, high, acc, acc2)


def fourth_other_kernel(q_ref, bias_ref, low_ref, high_ref, acc_in, acc_ref, kx_ref, vx_ref):
    both_tiles(3, bias_ref, low_ref, high_ref, kx_ref, vx_ref, ((q_ref, acc_ref),))


def attend_fourth_other(q2, bias, low, high, acc2):
    return pl.pallas_call(
        fourth_other_kernel,
        out_shape=ACC,
        in_specs=[VMEM] * 5,
        out_specs=VMEM,
        scratch_shapes=SPLIT,
        input_output_aliases={4: 0},
        compiler_params=PARAMS,
        cost_estimate=cost(2 * NK),
        name="attend_fourth_other",
    )(q2, bias, low, high, acc2)


HALF = NQ // 2
SUMS = 16


def split_last(low_ref, high_ref, bias_ref):
    return split_kv(jnp.concatenate([low_ref[...], high_ref[...]], axis=0), NZ // 2, bias_ref)


def last_other_kernel(q_ref, bias_ref, low_ref, high_ref, in_ref, message_ref, acc_ref):
    def store(rows, part):
        acc_ref[rows, :] = in_ref[rows, :] + part

    tile(q_ref, *split_last(low_ref, high_ref, bias_ref), store)
    lane = lax.broadcasted_iota(jnp.int32, (BLOCK, 128), 1)
    row = lax.broadcasted_iota(jnp.int32, (SUMS, 128), 0)
    column = lax.broadcasted_iota(jnp.int32, (SUMS, 128), 1)
    sums = jnp.zeros((SUMS, BLOCK), F32)
    blocks = [acc_ref[n * BLOCK : (n + 1) * BLOCK, :] for n in range(8)]
    for m in range(NY):
        pair = jnp.where(lane < HD, pltpu.roll(blocks[2 * m], 64, 1), blocks[2 * m + 1])
        message_ref[m * BLOCK : (m + 1) * BLOCK, :] = pair.astype(BF16)
    for n in range(8):
        coarse = blocks[n].astype(BF16).astype(F32)
        spread = jnp.where(lane == 0, coarse, jnp.where(lane == 1, blocks[n] - coarse, 0.0)).astype(BF16)
        at = jnp.where((row // 2 == n) & (row % 2 == column), 1.0, 0.0).astype(BF16)
        sums += lax.dot_general(at, spread, (((1,), (1,)), ((), ())), preferred_element_type=F32)
    message_ref[HALF:, :] = sums.astype(BF16)


def attend_last_other(q2, bias, low, high, acc2):
    return pl.pallas_call(
        last_other_kernel,
        out_shape=jax.ShapeDtypeStruct((HALF + SUMS, 128), BF16),
        in_specs=[VMEM] * 5,
        out_specs=VMEM,
        scratch_shapes=[pltpu.VMEM((NQ, 128), F32)],
        compiler_params=PARAMS,
        cost_estimate=cost(NK),
        name="attend_last_other",
    )(q2, bias, low, high, acc2)


def last_mine_kernel(q_ref, bias_ref, low_ref, high_ref, far_low, far_high, acc_in, acc_ref, kx_ref, vx_ref):
    both_tiles(3, bias_ref, low_ref, high_ref, kx_ref, vx_ref, ((q_ref, acc_ref),))
    tile(q_ref, *split_last(far_low, far_high, bias_ref), add(acc_ref))


def attend_last_mine(q, bias, low, high, far_low, far_high, acc):
    return pl.pallas_call(
        last_mine_kernel,
        out_shape=ACC,
        in_specs=[VMEM] * 7,
        out_specs=VMEM,
        scratch_shapes=SPLIT,
        input_output_aliases={6: 0},
        compiler_params=PARAMS,
        cost_estimate=cost(3 * NK),
        name="attend_last_mine",
    )(q, bias, low, high, far_low, far_high, acc)


def finish_kernel(mine_ref, message_ref, *out_refs):
    lane = lax.broadcasted_iota(jnp.int32, (BLOCK, 128), 1)
    row = lax.broadcasted_iota(jnp.int32, (SUMS, 128), 0)
    sums = message_ref[HALF:, :]
    blocks = [mine_ref[n * BLOCK : (n + 1) * BLOCK, :] for n in range(8)]
    spread = []
    for n in range(8):
        at = jnp.where(row // 2 == n, 1.0, 0.0).astype(BF16)
        spread.append(lax.dot_general(sums, at, (((0,), (0,)), ((), ())), preferred_element_type=F32))
    for m in range(NY):
        one, two = blocks[2 * m], blocks[2 * m + 1]
        total = jnp.where(lane < HD, pltpu.roll(one, 64, 1), two)
        total += message_ref[m * BLOCK : (m + 1) * BLOCK, :].astype(F32)
        weight = jnp.where(lane < HD, one + spread[2 * m], pltpu.roll(two, 64, 1) + spread[2 * m + 1])
        out_refs[m][...] = (total / weight).astype(BF16)


def finish(mine, message):
    return pl.pallas_call(
        finish_kernel,
        out_shape=[jax.ShapeDtypeStruct((BLOCK, 128), BF16)] * NY,
        in_specs=[VMEM, VMEM],
        out_specs=[VMEM] * NY,
        compiler_params=PARAMS,
        name="finish",
    )(mine, message)


def output_kernel(a_ref, own_ref, near_ref, far_ref, out_ref, w_ref):
    y, xl, core = (lax.axis_index(a).astype(jnp.int32) for a in ("y", "xl", "core"))
    for side, turn, piece in (
        (xl, core, own_ref[...]),
        (xl, 1 - core, near_ref[...]),
        (1 - xl, core, far_ref[:256, :]),
        (1 - xl, 1 - core, far_ref[256:, :]),
    ):
        w_ref[pl.ds(pl.multiple_of((2 * side + turn) * 256, 256), 256), :] = piece
    lane = lax.broadcasted_iota(jnp.int32, (BLOCK, 128), 1)
    tops, bottoms, weights = [], [], []
    for source in range(4):
        for s in range(0, NY, 2):
            one, two = a_ref[4 * source + s].astype(F32), a_ref[4 * source + s + 1].astype(F32)
            tops.append(jnp.where(lane < HD, one, pltpu.roll(two, 64, 1)).astype(BF16))
            bottoms.append(jnp.where(lane < HD, pltpu.roll(one, 64, 1), two).astype(BF16))
            for at in (s, s + 1):
                row = source * 256 + lax.rem(y + at, NY) * HD
                weights.append(w_ref[pl.ds(pl.multiple_of(row, HD), HD), :])
    features = jnp.concatenate([jnp.concatenate(tops, axis=1), jnp.concatenate(bottoms, axis=1)], axis=0)
    out_ref[...] = jnp.dot(features, jnp.concatenate(weights, axis=0), preferred_element_type=F32).astype(BF16)


def output(attended, own, near, far):
    return pl.pallas_call(
        output_kernel,
        out_shape=jax.ShapeDtypeStruct((ROWS, 256), BF16),
        in_specs=[VMEM] * 4,
        out_specs=VMEM,
        scratch_shapes=[pltpu.VMEM((1024, 256), BF16)],
        compiler_params=PARAMS,
        name="output",
    )(attended, own, near, far)


def shards(tokens, gain, w_query, w_key, w_value, w_out, temper, adjacency, order):
    whole = lax.all_gather(tokens, HEAD, axis=1, tiled=True)
    messages = project(whole, gain[None, :], w_query, w_key, w_value, temper)
    xl, core = lax.axis_index("xl"), lax.axis_index("core")
    w_out, messages = lax.optimization_barrier((w_out, messages))
    block = lambda side, turn: lax.dynamic_slice_in_dim(w_out, (2 * side + turn) * 256, 256, 1)
    own, relayed = block(xl, core), block(1 - xl, core)
    near = jnp.concatenate([block(xl, 1 - core), block(1 - xl, 1 - core)], axis=0)
    near = lax.ppermute(near, "core", ring(NCORE, 1))
    turned = {s: lax.ppermute(messages[s], "y", ring(NY, s)) for s in (2, 1, 3)}
    got = jnp.stack([messages[0]] + [turned[s] for s in range(1, NY)])
    kv = got[:, :ROWS, :].reshape(NK, 128)
    query = got[:, ROWS:, :]
    query, kv, near = lax.optimization_barrier((query, kv, near))
    up = lambda part: lax.ppermute(part, "z", ring(NZ, 1))
    down = lambda part: lax.ppermute(part, "z", ring(NZ, -1))
    low, high = up(kv), down(kv)
    other = lax.ppermute(query, "xh", ring(NXH, 1))
    q, bias, acc = attend_first(order, adjacency, query, kv)
    low, high, acc = lax.optimization_barrier((low, high, acc))
    low2, high2 = up(low), down(high)
    q2, acc, acc2 = attend_second(q, other, bias, low, high, acc)
    low2, high2, acc, near = lax.optimization_barrier((low2, high2, acc, near))
    low3, high3 = up(low2), down(high2)
    far = lax.ppermute(jnp.concatenate([relayed, near[256:]], axis=0), "xl", ring(NXL, 1))
    acc, acc2 = attend_third(q, q2, bias, kv, low2, high2, acc, acc2)
    low3, high3, acc2 = lax.optimization_barrier((low3, high3, acc2))
    low4, high4 = up(low3[: NK // 2]), down(high3[NK // 2 :])
    acc2 = attend_fourth_other(q2, bias, low3, high3, acc2)
    low4, high4, acc2, far = lax.optimization_barrier((low4, high4, acc2, far))
    message = attend_last_other(q2, bias, low4, high4, acc2)
    message, acc = lax.optimization_barrier((message, acc))
    message = lax.ppermute(message, "xh", ring(NXH, 1))
    attended = finish(attend_last_mine(q, bias, low3, high3, low4, high4, acc), message)
    back = jnp.stack([attended[0]] + [lax.ppermute(attended[s], "y", ring(NY, -s)) for s in range(1, NY)])
    gathered = lax.all_gather(back, HEAD, axis=0, tiled=True)
    return output(gathered, own, near[:256], far)


def solution(mesh):
    fine = Mesh(mesh.devices.reshape(NXH, NZ, NY, NXL, NCORE), CTX + HEAD)
    in_specs = (
        P(CTX, HEAD),
        P(),
        P(None, HEAD),
        P(None, HEAD),
        P(None, HEAD),
        P(HEAD, None),
        P(HEAD),
        P(),
        P(),
    )
    return jax.shard_map(shards, mesh=fine, in_specs=in_specs, out_specs=P(CTX, HEAD), check_vma=False)
```

```python
import jax
import jax.numpy as jnp
from jax import lax
from jax.experimental import pallas as pl
from jax.experimental.pallas import tpu as pltpu
from jax.sharding import Mesh, PartitionSpec as P

CTX = ("xh", "z", "y")
HEAD = ("xl", "core")
NXH, NZ, NY, NXL, NCORE = 2, 8, 4, 2, 2
ORDER = (0, 2, 1, 3)
BLOCK = 128
HD = 64
ROWS = 256
EPS = 1e-06
LOG2E = 1.4426950408889634
DEAD = -30000.0
F32 = jnp.float32
BF16 = jnp.bfloat16
VMEM = pl.BlockSpec(memory_space=pltpu.VMEM)
SMEM = pl.BlockSpec(memory_space=pltpu.SMEM)
HBM = pl.BlockSpec(memory_space=pltpu.HBM)
PARAMS = pltpu.CompilerParams(vmem_limit_bytes=32 << 20)


def ring(length, by):
    return [(i, (i + by) % length) for i in range(length)]


def project_kernel(
    x_ref, temper_hbm, gain_hbm, wq_hbm, wk_hbm, wv_hbm, *refs
):
    out_refs, (stage_ref, temper_ref, gain_ref, wq_ref, wk_ref, wv_ref, sems) = refs[:NY], refs[NY:]
    pairs = (
        (gain_hbm, gain_ref),
        (wq_hbm, wq_ref),
        (wk_hbm, wk_ref),
        (wv_hbm, wv_ref),
        (temper_hbm, temper_ref),
    )
    copies = [pltpu.make_async_copy(source, target, sems.at[n]) for n, (source, target) in enumerate(pairs)]
    for copy in copies:
        copy.start()
    x = x_ref[...].astype(F32)
    scaled = x * lax.rsqrt(jnp.mean(x * x, axis=-1, keepdims=True) + EPS)
    copies[0].wait()
    normed = (scaled * gain_ref[...]).astype(BF16)
    copies[1].wait()
    query = jnp.dot(normed, wq_ref[...], preferred_element_type=F32)
    copies[2].wait()
    keys = jnp.dot(normed, wk_ref[...], preferred_element_type=F32)
    copies[3].wait()
    values = jnp.dot(normed, wv_ref[...], preferred_element_type=F32)

    copies[4].wait()

    lower = lax.broadcasted_iota(jnp.int32, (ROWS, 128), 1) < HD
    head = lower[:BLOCK]

    def unit(pair, first=1.0, second=1.0):
        square = pair * pair
        low = jnp.sum(jnp.where(lower, square, 0.0), axis=-1, keepdims=True)
        high = jnp.sum(jnp.where(lower, 0.0, square), axis=-1, keepdims=True)
        low = lax.rsqrt(low / HD + EPS) * first
        high = lax.rsqrt(high / HD + EPS) * second
        return pair * jnp.where(lower, low, high)

    for n in range(2):
        j = 2 * n
        cols = slice(128 * n, 128 * (n + 1))
        q = unit(query[:, cols], temper_ref[j] * (LOG2E / HD), temper_ref[j + 1] * (LOG2E / HD))
        k = unit(keys[:, cols])
        v = values[:, cols]
        stage_ref[j, :ROWS, :] = jnp.where(lower, k, pltpu.roll(v, 64, 1)).astype(BF16)
        stage_ref[j + 1, :ROWS, :] = jnp.where(lower, pltpu.roll(k, 64, 1), v).astype(BF16)
        one, two = q[:BLOCK], q[BLOCK:]
        stage_ref[j, ROWS:, :] = jnp.where(head, one, pltpu.roll(two, 64, 1)).astype(BF16)
        stage_ref[j + 1, ROWS:, :] = jnp.where(head, pltpu.roll(one, 64, 1), two).astype(BF16)
    y = lax.axis_index("y").astype(jnp.int32)
    for s in range(NY):
        out_refs[s][...] = stage_ref[lax.rem(y + s, NY)]


def project(whole, gain, w_query, w_key, w_value, temper):
    hold = lambda x: pltpu.with_memory_space_constraint(x, pltpu.HBM)
    return pl.pallas_call(
        project_kernel,
        out_shape=[jax.ShapeDtypeStruct((ROWS + BLOCK, 128), BF16)] * NY,
        in_specs=[VMEM, HBM, HBM, HBM, HBM, HBM],
        out_specs=[VMEM] * NY,
        scratch_shapes=[
            pltpu.VMEM((NY, ROWS + BLOCK, 128), BF16),
            pltpu.SMEM((4,), F32),
            pltpu.VMEM((1, 1024), F32),
            pltpu.VMEM((1024, 256), BF16),
            pltpu.VMEM((1024, 256), BF16),
            pltpu.VMEM((1024, 256), BF16),
            pltpu.SemaphoreType.DMA((5,)),
        ],
        compiler_params=PARAMS,
        name="project",
    )(whole, hold(temper), hold(gain), hold(w_query), hold(w_key), hold(w_value))


QT = 256
NQ = 1024
NK = 1024


def widen(packed_ref, first, out_ref):
    lane = lax.broadcasted_iota(jnp.int32, (BLOCK, 128), 1)
    for m in range(NY):
        pair = packed_ref[m].astype(F32)
        for b in range(2):
            part = pair if b == 0 else pltpu.roll(pair, 64, 1)
            flag = jnp.where(lane == HD + first + 2 * m + b, 1.0, 0.0)
            at = (2 * m + b) * BLOCK
            out_ref[at : at + BLOCK, :] = jnp.where(lane < HD, part, flag).astype(BF16)


def bias_rows(order_ref, adjacency_ref, keys_ref, queries_ref, bias_ref):
    z, y, xh = (lax.axis_index(a).astype(jnp.int32) for a in ("z", "y", "xh"))
    lane = lax.broadcasted_iota(jnp.int32, (1, 128), 1)

    def pick(side, zs, s, b):
        block = 2 * ((side * NZ + zs) * NY + lax.rem(y - s + NY, NY)) + b
        return jnp.where(lane == order_ref[block], 1.0, 0.0)

    queries_ref[...] = jnp.zeros_like(queries_ref)
    for i, s in enumerate(ORDER):
        for b in range(2):
            n = 2 * i + b
            queries_ref[HD + n : HD + n + 1, :] = pick(xh, z, s, b)
            queries_ref[HD + 8 + n : HD + 9 + n, :] = pick(1 - xh, z, s, b)
            for zs in range(NZ):
                keys_ref[8 * zs + n : 8 * zs + n + 1, :] = pick(xh, zs, s, b)
    turned = (((1,), (1,)), ((), ()))
    adjacency = adjacency_ref[...].astype(F32).astype(BF16)
    keys, queries = keys_ref[...].astype(BF16), queries_ref[...].astype(BF16)
    picked = lax.dot_general(keys, adjacency, turned, preferred_element_type=F32).astype(BF16)
    live = lax.dot_general(picked, queries, turned, preferred_element_type=F32)
    bias_ref[...] = jnp.where(live > 0.5, 0.0, DEAD).reshape(NZ, NK // BLOCK, 128)


def chunk_at(distance):
    return lax.rem(lax.axis_index("z").astype(jnp.int32) + (distance + NZ), NZ)


def split_kv(kv, distance, bias_ref):
    lane = lax.broadcasted_iota(jnp.int32, (NK, 128), 1)
    kv = kv.astype(F32)
    table = bias_ref[chunk_at(distance)]
    bias = jnp.concatenate(
        [jnp.broadcast_to(table[b : b + 1, :], (BLOCK, 128)) for b in range(NK // BLOCK)], axis=0
    )
    return jnp.where(lane < HD, kv, bias).astype(BF16), jnp.where(lane < HD, 1.0, kv).astype(BF16)


def tile(q_ref, kx, vx, store):
    for t in range(NQ // QT):
        rows = slice(t * QT, (t + 1) * QT)
        scores = lax.dot_general(q_ref[rows, :], kx, (((1,), (1,)), ((), ())), preferred_element_type=F32)
        probs = jnp.exp2(scores).astype(BF16)
        store(rows, jnp.dot(probs, vx, preferred_element_type=F32))


def put(ref):
    def store(rows, part):
        ref[rows, :] = part

    return store


def add(ref):
    def store(rows, part):
        ref[rows, :] += part

    return store


def cost(keys):
    return pl.CostEstimate(flops=512 * NQ * keys, transcendentals=NQ * keys, bytes_accessed=4 << 20)


ACC = jax.ShapeDtypeStruct((NQ, 128), F32)
WIDE = jax.ShapeDtypeStruct((NQ, 128), BF16)


def first_kernel(order_ref, adjacency_ref, mine_ref, kv_ref, q_ref, bias_ref, acc_ref, keys_ref, queries_ref):
    bias_rows(order_ref, adjacency_ref, keys_ref, queries_ref, bias_ref)
    widen(mine_ref, 0, q_ref)
    kx, vx = split_kv(kv_ref[...], 0, bias_ref)
    tile(q_ref, kx, vx, put(acc_ref))


def attend_first(order, adjacency, mine, kv):
    return pl.pallas_call(
        first_kernel,
        out_shape=(WIDE, jax.ShapeDtypeStruct((NZ, NK // BLOCK, 128), F32), ACC),
        in_specs=[SMEM, VMEM, VMEM, VMEM],
        out_specs=(VMEM, VMEM, VMEM),
        scratch_shapes=[pltpu.VMEM((64, 128), F32), pltpu.VMEM((128, 128), F32)],
        compiler_params=PARAMS,
        cost_estimate=cost(NK),
        name="attend_first",
    )(order, adjacency, mine, kv)


def both_tiles(step, bias_ref, low_ref, high_ref, kx_ref, vx_ref, pairs):
    kx_ref[:NK, :], vx_ref[:NK, :] = split_kv(low_ref[...], -step, bias_ref)
    kx_ref[NK:, :], vx_ref[NK:, :] = split_kv(high_ref[...], step, bias_ref)
    for q_ref, acc_ref in pairs:
        tile(q_ref, kx_ref[...], vx_ref[...], add(acc_ref))


SPLIT = [pltpu.VMEM((2 * NK, 128), BF16), pltpu.VMEM((2 * NK, 128), BF16)]


def second_kernel(q_ref, other_ref, bias_ref, low_ref, high_ref, acc_in, q2_ref, acc_ref, acc2_ref, kx_ref, vx_ref):
    widen(other_ref, 8, q2_ref)
    acc2_ref[...] = jnp.zeros_like(acc2_ref)
    both_tiles(1, bias_ref, low_ref, high_ref, kx_ref, vx_ref, ((q_ref, acc_ref), (q2_ref, acc2_ref)))


def attend_second(q, other, bias, low, high, acc):
    return pl.pallas_call(
        second_kernel,
        out_shape=(WIDE, ACC, ACC),
        in_specs=[VMEM] * 6,
        out_specs=(VMEM, VMEM, VMEM),
        scratch_shapes=SPLIT,
        input_output_aliases={5: 1},
        compiler_params=PARAMS,
        cost_estimate=cost(4 * NK),
        name="attend_second",
    )(q, other, bias, low, high, acc)


def third_kernel(q_ref, q2_ref, bias_ref, kv_ref, low_ref, high_ref, in1, in2, acc_ref, acc2_ref, kx_ref, vx_ref):
    both_tiles(2, bias_ref, low_ref, high_ref, kx_ref, vx_ref, ((q_ref, acc_ref), (q2_ref, acc2_ref)))
    tile(q2_ref, *split_kv(kv_ref[...], 0, bias_ref), add(acc2_ref))


def attend_third(q, q2, bias, kv, low, high, acc, acc2):
    return pl.pallas_call(
        third_kernel,
        out_shape=(ACC, ACC),
        in_specs=[VMEM] * 8,
        out_specs=(VMEM, VMEM),
        scratch_shapes=SPLIT,
        input_output_aliases={6: 0, 7: 1},
        compiler_params=PARAMS,
        cost_estimate=cost(5 * NK),
        name="attend_third",
    )(q, q2, bias, kv, low, high, acc, acc2)


def fourth_other_kernel(q_ref, bias_ref, low_ref, high_ref, acc_in, acc_ref, kx_ref, vx_ref):
    both_tiles(3, bias_ref, low_ref, high_ref, kx_ref, vx_ref, ((q_ref, acc_ref),))


def attend_fourth_other(q2, bias, low, high, acc2):
    return pl.pallas_call(
        fourth_other_kernel,
        out_shape=ACC,
        in_specs=[VMEM] * 5,
        out_specs=VMEM,
        scratch_shapes=SPLIT,
        input_output_aliases={4: 0},
        compiler_params=PARAMS,
        cost_estimate=cost(2 * NK),
        name="attend_fourth_other",
    )(q2, bias, low, high, acc2)


HALF = NQ // 2
SUMS = 16


def split_last(low_ref, high_ref, bias_ref):
    return split_kv(jnp.concatenate([low_ref[...], high_ref[...]], axis=0), NZ // 2, bias_ref)


def last_other_kernel(q_ref, bias_ref, low_ref, high_ref, in_ref, message_ref, acc_ref):
    def store(rows, part):
        acc_ref[rows, :] = in_ref[rows, :] + part

    tile(q_ref, *split_last(low_ref, high_ref, bias_ref), store)
    lane = lax.broadcasted_iota(jnp.int32, (BLOCK, 128), 1)
    row = lax.broadcasted_iota(jnp.int32, (SUMS, 128), 0)
    column = lax.broadcasted_iota(jnp.int32, (SUMS, 128), 1)
    sums = jnp.zeros((SUMS, BLOCK), F32)
    blocks = [acc_ref[n * BLOCK : (n + 1) * BLOCK, :] for n in range(8)]
    for m in range(NY):
        pair = jnp.where(lane < HD, pltpu.roll(blocks[2 * m], 64, 1), blocks[2 * m + 1])
        message_ref[m * BLOCK : (m + 1) * BLOCK, :] = pair.astype(BF16)
    for n in range(8):
        coarse = blocks[n].astype(BF16).astype(F32)
        spread = jnp.where(lane == 0, coarse, jnp.where(lane == 1, blocks[n] - coarse, 0.0)).astype(BF16)
        at = jnp.where((row // 2 == n) & (row % 2 == column), 1.0, 0.0).astype(BF16)
        sums += lax.dot_general(at, spread, (((1,), (1,)), ((), ())), preferred_element_type=F32)
    message_ref[HALF:, :] = sums.astype(BF16)


def attend_last_other(q2, bias, low, high, acc2):
    return pl.pallas_call(
        last_other_kernel,
        out_shape=jax.ShapeDtypeStruct((HALF + SUMS, 128), BF16),
        in_specs=[VMEM] * 5,
        out_specs=VMEM,
        scratch_shapes=[pltpu.VMEM((NQ, 128), F32)],
        compiler_params=PARAMS,
        cost_estimate=cost(NK),
        name="attend_last_other",
    )(q2, bias, low, high, acc2)


def last_mine_kernel(q_ref, bias_ref, low_ref, high_ref, far_low, far_high, acc_in, acc_ref, kx_ref, vx_ref):
    both_tiles(3, bias_ref, low_ref, high_ref, kx_ref, vx_ref, ((q_ref, acc_ref),))
    tile(q_ref, *split_last(far_low, far_high, bias_ref), add(acc_ref))


def attend_last_mine(q, bias, low, high, far_low, far_high, acc):
    return pl.pallas_call(
        last_mine_kernel,
        out_shape=ACC,
        in_specs=[VMEM] * 7,
        out_specs=VMEM,
        scratch_shapes=SPLIT,
        input_output_aliases={6: 0},
        compiler_params=PARAMS,
        cost_estimate=cost(3 * NK),
        name="attend_last_mine",
    )(q, bias, low, high, far_low, far_high, acc)


def finish_kernel(mine_ref, message_ref, *out_refs):
    lane = lax.broadcasted_iota(jnp.int32, (BLOCK, 128), 1)
    row = lax.broadcasted_iota(jnp.int32, (SUMS, 128), 0)
    sums = message_ref[HALF:, :]
    blocks = [mine_ref[n * BLOCK : (n + 1) * BLOCK, :] for n in range(8)]
    spread = []
    for n in range(8):
        at = jnp.where(row // 2 == n, 1.0, 0.0).astype(BF16)
        spread.append(lax.dot_general(sums, at, (((0,), (0,)), ((), ())), preferred_element_type=F32))
    for m in range(NY):
        one, two = blocks[2 * m], blocks[2 * m + 1]
        total = jnp.where(lane < HD, pltpu.roll(one, 64, 1), two)
        total += message_ref[m * BLOCK : (m + 1) * BLOCK, :].astype(F32)
        weight = jnp.where(lane < HD, one + spread[2 * m], pltpu.roll(two, 64, 1) + spread[2 * m + 1])
        out_refs[m][...] = (total / weight).astype(BF16)


def finish(mine, message):
    return pl.pallas_call(
        finish_kernel,
        out_shape=[jax.ShapeDtypeStruct((BLOCK, 128), BF16)] * NY,
        in_specs=[VMEM, VMEM],
        out_specs=[VMEM] * NY,
        compiler_params=PARAMS,
        name="finish",
    )(mine, message)


def output_kernel(a_ref, own_ref, near_ref, far_ref, out_ref, w_ref):
    y, xl, core = (lax.axis_index(a).astype(jnp.int32) for a in ("y", "xl", "core"))
    for side, turn, piece in (
        (xl, core, own_ref[...]),
        (xl, 1 - core, near_ref[...]),
        (1 - xl, core, far_ref[:256, :]),
        (1 - xl, 1 - core, far_ref[256:, :]),
    ):
        w_ref[pl.ds(pl.multiple_of((2 * side + turn) * 256, 256), 256), :] = piece
    lane = lax.broadcasted_iota(jnp.int32, (BLOCK, 128), 1)
    tops, bottoms, weights = [], [], []
    for source in range(4):
        for s in range(0, NY, 2):
            one, two = a_ref[4 * source + s].astype(F32), a_ref[4 * source + s + 1].astype(F32)
            tops.append(jnp.where(lane < HD, one, pltpu.roll(two, 64, 1)).astype(BF16))
            bottoms.append(jnp.where(lane < HD, pltpu.roll(one, 64, 1), two).astype(BF16))
            for at in (s, s + 1):
                row = source * 256 + lax.rem(y + ORDER[at], NY) * HD
                weights.append(w_ref[pl.ds(pl.multiple_of(row, HD), HD), :])
    features = jnp.concatenate([jnp.concatenate(tops, axis=1), jnp.concatenate(bottoms, axis=1)], axis=0)
    out_ref[...] = jnp.dot(features, jnp.concatenate(weights, axis=0), preferred_element_type=F32).astype(BF16)


def output(attended, own, near, far):
    return pl.pallas_call(
        output_kernel,
        out_shape=jax.ShapeDtypeStruct((ROWS, 256), BF16),
        in_specs=[VMEM] * 4,
        out_specs=VMEM,
        scratch_shapes=[pltpu.VMEM((1024, 256), BF16)],
        compiler_params=PARAMS,
        name="output",
    )(attended, own, near, far)


def shards(tokens, gain, w_query, w_key, w_value, w_out, temper, adjacency, order):
    whole = lax.all_gather(tokens, HEAD, axis=1, tiled=True)
    messages = project(whole, gain[None, :], w_query, w_key, w_value, temper)
    xl, core = lax.axis_index("xl"), lax.axis_index("core")
    w_out, messages = lax.optimization_barrier((w_out, messages))
    block = lambda side, turn: lax.dynamic_slice_in_dim(w_out, (2 * side + turn) * 256, 256, 1)
    own, relayed = block(xl, core), block(1 - xl, core)
    near = jnp.concatenate([block(xl, 1 - core), block(1 - xl, 1 - core)], axis=0)
    near = lax.ppermute(near, "core", ring(NCORE, 1))
    got = jnp.stack([messages[s] if s == 0 else lax.ppermute(messages[s], "y", ring(NY, s)) for s in ORDER])
    kv = got[:, :ROWS, :].reshape(NK, 128)
    query = got[:, ROWS:, :]
    query, kv, near = lax.optimization_barrier((query, kv, near))
    up = lambda part: lax.ppermute(part, "z", ring(NZ, 1))
    down = lambda part: lax.ppermute(part, "z", ring(NZ, -1))
    low, high = up(kv), down(kv)
    other = lax.ppermute(query, "xh", ring(NXH, 1))
    q, bias, acc = attend_first(order, adjacency, query, kv)
    low, high, acc = lax.optimization_barrier((low, high, acc))
    low2, high2 = up(low), down(high)
    q2, acc, acc2 = attend_second(q, other, bias, low, high, acc)
    low2, high2, acc, near = lax.optimization_barrier((low2, high2, acc, near))
    low3, high3 = up(low2), down(high2)
    far = lax.ppermute(jnp.concatenate([relayed, near[256:]], axis=0), "xl", ring(NXL, 1))
    acc, acc2 = attend_third(q, q2, bias, kv, low2, high2, acc, acc2)
    low3, high3, acc2 = lax.optimization_barrier((low3, high3, acc2))
    low4, high4 = up(low3[: NK // 2]), down(high3[NK // 2 :])
    acc2 = attend_fourth_other(q2, bias, low3, high3, acc2)
    low4, high4, acc2, far = lax.optimization_barrier((low4, high4, acc2, far))
    message = attend_last_other(q2, bias, low4, high4, acc2)
    message, acc = lax.optimization_barrier((message, acc))
    message = lax.ppermute(message, "xh", ring(NXH, 1))
    attended = finish(attend_last_mine(q, bias, low3, high3, low4, high4, acc), message)
    back = jnp.stack([a if s == 0 else lax.ppermute(a, "y", ring(NY, -s)) for a, s in zip(attended, ORDER)])
    gathered = lax.all_gather(back, HEAD, axis=0, tiled=True)
    return output(gathered, own, near[:256], far)


def solution(mesh):
    fine = Mesh(mesh.devices.reshape(NXH, NZ, NY, NXL, NCORE), CTX + HEAD)
    in_specs = (
        P(CTX, HEAD),
        P(),
        P(None, HEAD),
        P(None, HEAD),
        P(None, HEAD),
        P(HEAD, None),
        P(HEAD),
        P(),
        P(),
    )
    return jax.shard_map(shards, mesh=fine, in_specs=in_specs, out_specs=P(CTX, HEAD), check_vma=False)
```

```python
import jax
import jax.numpy as jnp
from jax import lax
from jax.experimental import pallas as pl
from jax.experimental.pallas import tpu as pltpu
from jax.sharding import Mesh, PartitionSpec as P

CTX = ("xh", "z", "y")
HEAD = ("xl", "core")
NXH, NZ, NY, NXL, NCORE = 2, 8, 4, 2, 2
ORDER = (0, 1, 3, 2)
BLOCK = 128
HD = 64
ROWS = 256
EPS = 1e-06
LOG2E = 1.4426950408889634
DEAD = -30000.0
F32 = jnp.float32
BF16 = jnp.bfloat16
VMEM = pl.BlockSpec(memory_space=pltpu.VMEM)
SMEM = pl.BlockSpec(memory_space=pltpu.SMEM)
HBM = pl.BlockSpec(memory_space=pltpu.HBM)
PARAMS = pltpu.CompilerParams(vmem_limit_bytes=32 << 20)


def ring(length, by):
    return [(i, (i + by) % length) for i in range(length)]


def project_kernel(
    x_ref, temper_hbm, gain_hbm, wq_hbm, wk_hbm, wv_hbm, *refs
):
    out_refs, (stage_ref, temper_ref, gain_ref, wq_ref, wk_ref, wv_ref, sems) = refs[:NY], refs[NY:]
    pairs = (
        (gain_hbm, gain_ref),
        (wq_hbm, wq_ref),
        (wk_hbm, wk_ref),
        (wv_hbm, wv_ref),
        (temper_hbm, temper_ref),
    )
    copies = [pltpu.make_async_copy(source, target, sems.at[n]) for n, (source, target) in enumerate(pairs)]
    for copy in copies:
        copy.start()
    x = x_ref[...].astype(F32)
    scaled = x * lax.rsqrt(jnp.mean(x * x, axis=-1, keepdims=True) + EPS)
    copies[0].wait()
    normed = (scaled * gain_ref[...]).astype(BF16)
    copies[1].wait()
    query = jnp.dot(normed, wq_ref[...], preferred_element_type=F32)
    copies[2].wait()
    keys = jnp.dot(normed, wk_ref[...], preferred_element_type=F32)
    copies[3].wait()
    values = jnp.dot(normed, wv_ref[...], preferred_element_type=F32)

    copies[4].wait()

    lower = lax.broadcasted_iota(jnp.int32, (ROWS, 128), 1) < HD
    head = lower[:BLOCK]

    def unit(pair, first=1.0, second=1.0):
        square = pair * pair
        low = jnp.sum(jnp.where(lower, square, 0.0), axis=-1, keepdims=True)
        high = jnp.sum(jnp.where(lower, 0.0, square), axis=-1, keepdims=True)
        low = lax.rsqrt(low / HD + EPS) * first
        high = lax.rsqrt(high / HD + EPS) * second
        return pair * jnp.where(lower, low, high)

    for n in range(2):
        j = 2 * n
        cols = slice(128 * n, 128 * (n + 1))
        q = unit(query[:, cols], temper_ref[j] * (LOG2E / HD), temper_ref[j + 1] * (LOG2E / HD))
        k = unit(keys[:, cols])
        v = values[:, cols]
        stage_ref[j, :ROWS, :] = jnp.where(lower, k, pltpu.roll(v, 64, 1)).astype(BF16)
        stage_ref[j + 1, :ROWS, :] = jnp.where(lower, pltpu.roll(k, 64, 1), v).astype(BF16)
        one, two = q[:BLOCK], q[BLOCK:]
        stage_ref[j, ROWS:, :] = jnp.where(head, one, pltpu.roll(two, 64, 1)).astype(BF16)
        stage_ref[j + 1, ROWS:, :] = jnp.where(head, pltpu.roll(one, 64, 1), two).astype(BF16)
    y = lax.axis_index("y").astype(jnp.int32)
    for s in range(NY):
        out_refs[s][...] = stage_ref[lax.rem(y + s, NY)]


def project(whole, gain, w_query, w_key, w_value, temper):
    hold = lambda x: pltpu.with_memory_space_constraint(x, pltpu.HBM)
    return pl.pallas_call(
        project_kernel,
        out_shape=[jax.ShapeDtypeStruct((ROWS + BLOCK, 128), BF16)] * NY,
        in_specs=[VMEM, HBM, HBM, HBM, HBM, HBM],
        out_specs=[VMEM] * NY,
        scratch_shapes=[
            pltpu.VMEM((NY, ROWS + BLOCK, 128), BF16),
            pltpu.SMEM((4,), F32),
            pltpu.VMEM((1, 1024), F32),
            pltpu.VMEM((1024, 256), BF16),
            pltpu.VMEM((1024, 256), BF16),
            pltpu.VMEM((1024, 256), BF16),
            pltpu.SemaphoreType.DMA((5,)),
        ],
        compiler_params=PARAMS,
        name="project",
    )(whole, hold(temper), hold(gain), hold(w_query), hold(w_key), hold(w_value))


QT = 256
NQ = 1024
NK = 1024


def widen(packed_ref, first, out_ref):
    lane = lax.broadcasted_iota(jnp.int32, (BLOCK, 128), 1)
    for m in range(NY):
        pair = packed_ref[m].astype(F32)
        for b in range(2):
            part = pair if b == 0 else pltpu.roll(pair, 64, 1)
            flag = jnp.where(lane == HD + first + 2 * m + b, 1.0, 0.0)
            at = (2 * m + b) * BLOCK
            out_ref[at : at + BLOCK, :] = jnp.where(lane < HD, part, flag).astype(BF16)


def bias_rows(order_ref, adjacency_ref, keys_ref, queries_ref, bias_ref):
    z, y, xh = (lax.axis_index(a).astype(jnp.int32) for a in ("z", "y", "xh"))
    lane = lax.broadcasted_iota(jnp.int32, (1, 128), 1)

    def pick(side, zs, s, b):
        block = 2 * ((side * NZ + zs) * NY + lax.rem(y - s + NY, NY)) + b
        return jnp.where(lane == order_ref[block], 1.0, 0.0)

    queries_ref[...] = jnp.zeros_like(queries_ref)
    for i, s in enumerate(ORDER):
        for b in range(2):
            n = 2 * i + b
            queries_ref[HD + n : HD + n + 1, :] = pick(xh, z, s, b)
            queries_ref[HD + 8 + n : HD + 9 + n, :] = pick(1 - xh, z, s, b)
            for zs in range(NZ):
                keys_ref[8 * zs + n : 8 * zs + n + 1, :] = pick(xh, zs, s, b)
    turned = (((1,), (1,)), ((), ()))
    adjacency = adjacency_ref[...].astype(F32).astype(BF16)
    keys, queries = keys_ref[...].astype(BF16), queries_ref[...].astype(BF16)
    picked = lax.dot_general(keys, adjacency, turned, preferred_element_type=F32).astype(BF16)
    live = lax.dot_general(picked, queries, turned, preferred_element_type=F32)
    bias_ref[...] = jnp.where(live > 0.5, 0.0, DEAD).reshape(NZ, NK // BLOCK, 128)


def chunk_at(distance):
    return lax.rem(lax.axis_index("z").astype(jnp.int32) + (distance + NZ), NZ)


def split_kv(kv, distance, bias_ref):
    lane = lax.broadcasted_iota(jnp.int32, (NK, 128), 1)
    kv = kv.astype(F32)
    table = bias_ref[chunk_at(distance)]
    bias = jnp.concatenate(
        [jnp.broadcast_to(table[b : b + 1, :], (BLOCK, 128)) for b in range(NK // BLOCK)], axis=0
    )
    return jnp.where(lane < HD, kv, bias).astype(BF16), jnp.where(lane < HD, 1.0, kv).astype(BF16)


def tile(q_ref, kx, vx, store):
    for t in range(NQ // QT):
        rows = slice(t * QT, (t + 1) * QT)
        scores = lax.dot_general(q_ref[rows, :], kx, (((1,), (1,)), ((), ())), preferred_element_type=F32)
        probs = jnp.exp2(scores).astype(BF16)
        store(rows, jnp.dot(probs, vx, preferred_element_type=F32))


def put(ref):
    def store(rows, part):
        ref[rows, :] = part

    return store


def add(ref):
    def store(rows, part):
        ref[rows, :] += part

    return store


def cost(keys):
    return pl.CostEstimate(flops=512 * NQ * keys, transcendentals=NQ * keys, bytes_accessed=4 << 20)


ACC = jax.ShapeDtypeStruct((NQ, 128), F32)
WIDE = jax.ShapeDtypeStruct((NQ, 128), BF16)


def first_kernel(order_ref, adjacency_ref, mine_ref, kv_ref, q_ref, bias_ref, acc_ref, keys_ref, queries_ref):
    bias_rows(order_ref, adjacency_ref, keys_ref, queries_ref, bias_ref)
    widen(mine_ref, 0, q_ref)
    kx, vx = split_kv(kv_ref[...], 0, bias_ref)
    tile(q_ref, kx, vx, put(acc_ref))


def attend_first(order, adjacency, mine, kv):
    return pl.pallas_call(
        first_kernel,
        out_shape=(WIDE, jax.ShapeDtypeStruct((NZ, NK // BLOCK, 128), F32), ACC),
        in_specs=[SMEM, VMEM, VMEM, VMEM],
        out_specs=(VMEM, VMEM, VMEM),
        scratch_shapes=[pltpu.VMEM((64, 128), F32), pltpu.VMEM((128, 128), F32)],
        compiler_params=PARAMS,
        cost_estimate=cost(NK),
        name="attend_first",
    )(order, adjacency, mine, kv)


def both_tiles(step, bias_ref, low_ref, high_ref, kx_ref, vx_ref, pairs):
    kx_ref[:NK, :], vx_ref[:NK, :] = split_kv(low_ref[...], -step, bias_ref)
    kx_ref[NK:, :], vx_ref[NK:, :] = split_kv(high_ref[...], step, bias_ref)
    for q_ref, acc_ref in pairs:
        tile(q_ref, kx_ref[...], vx_ref[...], add(acc_ref))


SPLIT = [pltpu.VMEM((2 * NK, 128), BF16), pltpu.VMEM((2 * NK, 128), BF16)]


def second_kernel(q_ref, other_ref, bias_ref, low_ref, high_ref, acc_in, q2_ref, acc_ref, acc2_ref, kx_ref, vx_ref):
    widen(other_ref, 8, q2_ref)
    acc2_ref[...] = jnp.zeros_like(acc2_ref)
    both_tiles(1, bias_ref, low_ref, high_ref, kx_ref, vx_ref, ((q_ref, acc_ref), (q2_ref, acc2_ref)))


def attend_second(q, other, bias, low, high, acc):
    return pl.pallas_call(
        second_kernel,
        out_shape=(WIDE, ACC, ACC),
        in_specs=[VMEM] * 6,
        out_specs=(VMEM, VMEM, VMEM),
        scratch_shapes=SPLIT,
        input_output_aliases={5: 1},
        compiler_params=PARAMS,
        cost_estimate=cost(4 * NK),
        name="attend_second",
    )(q, other, bias, low, high, acc)


def third_kernel(q_ref, q2_ref, bias_ref, kv_ref, low_ref, high_ref, in1, in2, acc_ref, acc2_ref, kx_ref, vx_ref):
    both_tiles(2, bias_ref, low_ref, high_ref, kx_ref, vx_ref, ((q_ref, acc_ref), (q2_ref, acc2_ref)))
    tile(q2_ref, *split_kv(kv_ref[...], 0, bias_ref), add(acc2_ref))


def attend_third(q, q2, bias, kv, low, high, acc, acc2):
    return pl.pallas_call(
        third_kernel,
        out_shape=(ACC, ACC),
        in_specs=[VMEM] * 8,
        out_specs=(VMEM, VMEM),
        scratch_shapes=SPLIT,
        input_output_aliases={6: 0, 7: 1},
        compiler_params=PARAMS,
        cost_estimate=cost(5 * NK),
        name="attend_third",
    )(q, q2, bias, kv, low, high, acc, acc2)


def fourth_other_kernel(q_ref, bias_ref, low_ref, high_ref, acc_in, acc_ref, kx_ref, vx_ref):
    both_tiles(3, bias_ref, low_ref, high_ref, kx_ref, vx_ref, ((q_ref, acc_ref),))


def attend_fourth_other(q2, bias, low, high, acc2):
    return pl.pallas_call(
        fourth_other_kernel,
        out_shape=ACC,
        in_specs=[VMEM] * 5,
        out_specs=VMEM,
        scratch_shapes=SPLIT,
        input_output_aliases={4: 0},
        compiler_params=PARAMS,
        cost_estimate=cost(2 * NK),
        name="attend_fourth_other",
    )(q2, bias, low, high, acc2)


HALF = NQ // 2
SUMS = 16


def split_last(low_ref, high_ref, bias_ref):
    return split_kv(jnp.concatenate([low_ref[...], high_ref[...]], axis=0), NZ // 2, bias_ref)


def last_other_kernel(q_ref, bias_ref, low_ref, high_ref, in_ref, message_ref, acc_ref):
    def store(rows, part):
        acc_ref[rows, :] = in_ref[rows, :] + part

    tile(q_ref, *split_last(low_ref, high_ref, bias_ref), store)
    lane = lax.broadcasted_iota(jnp.int32, (BLOCK, 128), 1)
    row = lax.broadcasted_iota(jnp.int32, (SUMS, 128), 0)
    column = lax.broadcasted_iota(jnp.int32, (SUMS, 128), 1)
    sums = jnp.zeros((SUMS, BLOCK), F32)
    blocks = [acc_ref[n * BLOCK : (n + 1) * BLOCK, :] for n in range(8)]
    for m in range(NY):
        pair = jnp.where(lane < HD, pltpu.roll(blocks[2 * m], 64, 1), blocks[2 * m + 1])
        message_ref[m * BLOCK : (m + 1) * BLOCK, :] = pair.astype(BF16)
    for n in range(8):
        coarse = blocks[n].astype(BF16).astype(F32)
        spread = jnp.where(lane == 0, coarse, jnp.where(lane == 1, blocks[n] - coarse, 0.0)).astype(BF16)
        at = jnp.where((row // 2 == n) & (row % 2 == column), 1.0, 0.0).astype(BF16)
        sums += lax.dot_general(at, spread, (((1,), (1,)), ((), ())), preferred_element_type=F32)
    message_ref[HALF:, :] = sums.astype(BF16)


def attend_last_other(q2, bias, low, high, acc2):
    return pl.pallas_call(
        last_other_kernel,
        out_shape=jax.ShapeDtypeStruct((HALF + SUMS, 128), BF16),
        in_specs=[VMEM] * 5,
        out_specs=VMEM,
        scratch_shapes=[pltpu.VMEM((NQ, 128), F32)],
        compiler_params=PARAMS,
        cost_estimate=cost(NK),
        name="attend_last_other",
    )(q2, bias, low, high, acc2)


def last_mine_kernel(q_ref, bias_ref, low_ref, high_ref, far_low, far_high, acc_in, acc_ref, kx_ref, vx_ref):
    both_tiles(3, bias_ref, low_ref, high_ref, kx_ref, vx_ref, ((q_ref, acc_ref),))
    tile(q_ref, *split_last(far_low, far_high, bias_ref), add(acc_ref))


def attend_last_mine(q, bias, low, high, far_low, far_high, acc):
    return pl.pallas_call(
        last_mine_kernel,
        out_shape=ACC,
        in_specs=[VMEM] * 7,
        out_specs=VMEM,
        scratch_shapes=SPLIT,
        input_output_aliases={6: 0},
        compiler_params=PARAMS,
        cost_estimate=cost(3 * NK),
        name="attend_last_mine",
    )(q, bias, low, high, far_low, far_high, acc)


def finish_kernel(mine_ref, message_ref, *out_refs):
    lane = lax.broadcasted_iota(jnp.int32, (BLOCK, 128), 1)
    row = lax.broadcasted_iota(jnp.int32, (SUMS, 128), 0)
    sums = message_ref[HALF:, :]
    blocks = [mine_ref[n * BLOCK : (n + 1) * BLOCK, :] for n in range(8)]
    spread = []
    for n in range(8):
        at = jnp.where(row // 2 == n, 1.0, 0.0).astype(BF16)
        spread.append(lax.dot_general(sums, at, (((0,), (0,)), ((), ())), preferred_element_type=F32))
    for m in range(NY):
        one, two = blocks[2 * m], blocks[2 * m + 1]
        total = jnp.where(lane < HD, pltpu.roll(one, 64, 1), two)
        total += message_ref[m * BLOCK : (m + 1) * BLOCK, :].astype(F32)
        weight = jnp.where(lane < HD, one + spread[2 * m], pltpu.roll(two, 64, 1) + spread[2 * m + 1])
        out_refs[m][...] = (total / weight).astype(BF16)


def finish(mine, message):
    return pl.pallas_call(
        finish_kernel,
        out_shape=[jax.ShapeDtypeStruct((BLOCK, 128), BF16)] * NY,
        in_specs=[VMEM, VMEM],
        out_specs=[VMEM] * NY,
        compiler_params=PARAMS,
        name="finish",
    )(mine, message)


def output_kernel(a_ref, own_ref, near_ref, far_ref, out_ref, w_ref):
    y, xl, core = (lax.axis_index(a).astype(jnp.int32) for a in ("y", "xl", "core"))
    for side, turn, piece in (
        (xl, core, own_ref[...]),
        (xl, 1 - core, near_ref[...]),
        (1 - xl, core, far_ref[:256, :]),
        (1 - xl, 1 - core, far_ref[256:, :]),
    ):
        w_ref[pl.ds(pl.multiple_of((2 * side + turn) * 256, 256), 256), :] = piece
    lane = lax.broadcasted_iota(jnp.int32, (BLOCK, 128), 1)
    tops, bottoms, weights = [], [], []
    for source in range(4):
        for s in range(0, NY, 2):
            one, two = a_ref[4 * source + s].astype(F32), a_ref[4 * source + s + 1].astype(F32)
            tops.append(jnp.where(lane < HD, one, pltpu.roll(two, 64, 1)).astype(BF16))
            bottoms.append(jnp.where(lane < HD, pltpu.roll(one, 64, 1), two).astype(BF16))
            for at in (s, s + 1):
                row = source * 256 + lax.rem(y + ORDER[at], NY) * HD
                weights.append(w_ref[pl.ds(pl.multiple_of(row, HD), HD), :])
    features = jnp.concatenate([jnp.concatenate(tops, axis=1), jnp.concatenate(bottoms, axis=1)], axis=0)
    out_ref[...] = jnp.dot(features, jnp.concatenate(weights, axis=0), preferred_element_type=F32).astype(BF16)


def output(attended, own, near, far):
    return pl.pallas_call(
        output_kernel,
        out_shape=jax.ShapeDtypeStruct((ROWS, 256), BF16),
        in_specs=[VMEM] * 4,
        out_specs=VMEM,
        scratch_shapes=[pltpu.VMEM((1024, 256), BF16)],
        compiler_params=PARAMS,
        name="output",
    )(attended, own, near, far)


def shards(tokens, gain, w_query, w_key, w_value, w_out, temper, adjacency, order):
    whole = lax.all_gather(tokens, HEAD, axis=1, tiled=True)
    messages = project(whole, gain[None, :], w_query, w_key, w_value, temper)
    xl, core = lax.axis_index("xl"), lax.axis_index("core")
    w_out, messages = lax.optimization_barrier((w_out, messages))
    block = lambda side, turn: lax.dynamic_slice_in_dim(w_out, (2 * side + turn) * 256, 256, 1)
    own, relayed = block(xl, core), block(1 - xl, core)
    near = jnp.concatenate([block(xl, 1 - core), block(1 - xl, 1 - core)], axis=0)
    near = lax.ppermute(near, "core", ring(NCORE, 1))
    got = jnp.stack([messages[s] if s == 0 else lax.ppermute(messages[s], "y", ring(NY, s)) for s in ORDER])
    kv = got[:, :ROWS, :].reshape(NK, 128)
    query = got[:, ROWS:, :]
    query, kv, near = lax.optimization_barrier((query, kv, near))
    up = lambda part: lax.ppermute(part, "z", ring(NZ, 1))
    down = lambda part: lax.ppermute(part, "z", ring(NZ, -1))
    low, high = up(kv), down(kv)
    other = lax.ppermute(query, "xh", ring(NXH, 1))
    q, bias, acc = attend_first(order, adjacency, query, kv)
    low, high, acc = lax.optimization_barrier((low, high, acc))
    low2, high2 = up(low), down(high)
    q2, acc, acc2 = attend_second(q, other, bias, low, high, acc)
    low2, high2, acc, near = lax.optimization_barrier((low2, high2, acc, near))
    low3, high3 = up(low2), down(high2)
    far = lax.ppermute(jnp.concatenate([relayed, near[256:]], axis=0), "xl", ring(NXL, 1))
    acc, acc2 = attend_third(q, q2, bias, kv, low2, high2, acc, acc2)
    low3, high3, acc2 = lax.optimization_barrier((low3, high3, acc2))
    low4, high4 = up(low3[: NK // 2]), down(high3[NK // 2 :])
    acc2 = attend_fourth_other(q2, bias, low3, high3, acc2)
    low4, high4, acc2, far = lax.optimization_barrier((low4, high4, acc2, far))
    message = attend_last_other(q2, bias, low4, high4, acc2)
    message, acc = lax.optimization_barrier((message, acc))
    message = lax.ppermute(message, "xh", ring(NXH, 1))
    attended = finish(attend_last_mine(q, bias, low3, high3, low4, high4, acc), message)
    back = jnp.stack([a if s == 0 else lax.ppermute(a, "y", ring(NY, -s)) for a, s in zip(attended, ORDER)])
    gathered = lax.all_gather(back, HEAD, axis=0, tiled=True)
    return output(gathered, own, near[:256], far)


def solution(mesh):
    fine = Mesh(mesh.devices.reshape(NXH, NZ, NY, NXL, NCORE), CTX + HEAD)
    in_specs = (
        P(CTX, HEAD),
        P(),
        P(None, HEAD),
        P(None, HEAD),
        P(None, HEAD),
        P(HEAD, None),
        P(HEAD),
        P(),
        P(),
    )
    return jax.shard_map(shards, mesh=fine, in_specs=in_specs, out_specs=P(CTX, HEAD), check_vma=False)
```
